512 devices in a mesh: mode: 16 (over x, y), patch: 32 (over z, core).
Axes of the slice: x: 4, y: 4, z: 16, core: 2. Of those that a mesh axis runs over, the one named last changes fastest.
Arguments:
- flow_speed: bfloat16 [3, 2, 1024, 32768], P(None, None, 'mode', 'patch'), may hold values from -6 to 6
- heat_state: float32 [2, 1024, 32768], P(None, 'mode', 'patch'), may hold values from -6 to 6
- planar_slope_matrices: bfloat16 [128, 2, 256, 256], P('patch'), may hold values from -0.25 to 0.25
- conduction_matrices: bfloat16 [128, 256, 256], P('patch'), as said below
- adjacent_partners: int32 [128, 4], P('patch'), may hold values from 0 to 20, as said below
- opposite_direction_flags: int32 [128, 4], P('patch'), may hold values from 0 to 1
- interpatch_sides: int32 [32, 4], P('patch'), may hold values from 0 to 15, as said below
- liquid_cells: int32 [32], P('patch'), may hold values from 2 to 4, as said below
Outputs:
- new_temperature: float32 [2, 1024, 32768], P(None, 'mode', 'patch')
The draws below stay inside these ranges and needn't reach their ends.
Inputs may be any that keep to these rules, and one draw needn't show every extreme that they name: `adjacent_partners`: element slots of a patch form a grid of 2 rows by 2 columns in an order drawn for each patch; partner faces are consistent both ways, walls across the chamber point at the zero trace. `interpatch_sides`: the first 2 entries name faces 0 of the first column, the rest faces 1 of the last column, by row. `liquid_cells`: some patch is fluid in all its elements. `conduction_matrices`: Symmetric; diagonal in 1 to 2, off-diagonal entries of magnitude at most 1 / sqrt(256).
All inputs are finite; a program needn't handle non-finite values.
Results may differ from the reference program's by a relative error of at most 0.0022.
Values may be sent and summed in bfloat16 or wider, within the bound.
A program may use at most 64 MiB of HBM per device.

```python
import math
import jax
import jax.numpy as jnp
from jax import lax

EDGE = 16
HARMONIC_NUMBER = 1024
ROWS = 2
COLS = 2
STEPS = 3
ELEMS = 4
NODES = 256
ZP = 3072
NPATCHES = 32
NE = 128
GRIDPOINT_SUM = 32768


def geometry(key):
    keys = jax.random.split(jax.random.fold_in(key, 11), NPATCHES)
    perm = jax.vmap(lambda k: jax.random.permutation(k, ELEMS))(keys).astype(jnp.int32)
    east = jax.random.randint(jax.random.fold_in(key, 12), (NPATCHES, ROWS, COLS), 0, 2).astype(jnp.int32)
    north = jax.random.randint(jax.random.fold_in(key, 13), (NPATCHES, ROWS, COLS), 0, 2).astype(jnp.int32)
    row_idx = jnp.broadcast_to(jnp.arange(ROWS, dtype=jnp.int32)[:, None], (ROWS, COLS))[None]
    col_idx = jnp.broadcast_to(jnp.arange(COLS, dtype=jnp.int32)[None, :], (ROWS, COLS))[None]
    grid = perm.reshape(NPATCHES, ROWS, COLS)
    wall = 4 * ELEMS + 2 * ROWS
    zeros = jnp.zeros_like(east)
    east_left = jnp.roll(east, 1, axis=2)
    nb0 = jnp.where(col_idx > 0, jnp.roll(grid, 1, axis=2) * 4 + 1, 4 * ELEMS + row_idx + zeros)
    fl0 = jnp.where(col_idx > 0, east_left, jnp.roll(east_left, 1, axis=0))
    nb1 = jnp.where(col_idx < COLS - 1, jnp.roll(grid, -1, axis=2) * 4, 4 * ELEMS + ROWS + row_idx + zeros)
    fl1 = east
    nb2 = jnp.where(row_idx > 0, jnp.roll(grid, 1, axis=1) * 4 + 3, wall + zeros)
    fl2 = jnp.where(row_idx > 0, jnp.roll(north, 1, axis=1), zeros)
    nb3 = jnp.where(row_idx < ROWS - 1, jnp.roll(grid, -1, axis=1) * 4 + 2, wall + zeros)
    fl3 = jnp.where(row_idx < ROWS - 1, north, zeros)
    nbr_pos = jnp.stack([nb0, nb1, nb2, nb3], axis=-1).reshape(NPATCHES, ELEMS, 4)
    flip_pos = jnp.stack([fl0, fl1, fl2, fl3], axis=-1).reshape(NPATCHES, ELEMS, 4)
    inverse = jnp.argsort(perm, axis=1).astype(jnp.int32)
    nbr = jnp.take_along_axis(nbr_pos, inverse[:, :, None], axis=1)
    flips = jnp.take_along_axis(flip_pos, inverse[:, :, None], axis=1)
    send = jnp.concatenate([grid[:, :, 0] * 4, grid[:, :, COLS - 1] * 4 + 1], axis=1)
    return (nbr.reshape(NE, 4).astype(jnp.int32), flips.reshape(NE, 4).astype(jnp.int32), send.astype(jnp.int32))


def draw_adjacent_partners(key, part):
    return geometry(key)[0]


def draw_opposite_direction_flags(key, part):
    return geometry(key)[1]


def draw_interpatch_sides(key, part):
    return geometry(key)[2]


def draw_liquid_cells(key, part):
    counts = jax.random.randint(jax.random.fold_in(key, 21), (NPATCHES,), ELEMS // 2, ELEMS + 1)
    busiest = jax.random.randint(jax.random.fold_in(key, 22), (), 0, NPATCHES)
    return jnp.where(jnp.arange(NPATCHES) == busiest, ELEMS, counts).astype(jnp.int32)


def draw_conduction_matrices(key, part):
    bound = 1.0 / math.sqrt(NODES)
    diag = jax.random.uniform(jax.random.fold_in(key, 31), (NE, NODES), jnp.float32, 1.0, 2.0)
    off = jax.random.uniform(jax.random.fold_in(key, 32), (NE, NODES, NODES), jnp.float32, -bound, bound)
    off = 0.5 * (off + jnp.swapaxes(off, 1, 2))
    eye = jnp.eye(NODES, dtype=jnp.float32)[None]
    full = off * (1.0 - eye) + eye * diag[:, :, None]
    return full.astype(jnp.bfloat16)


def steps_of(stream_key, shape, cuts, least, top_value):
    loudness = 1.0
    for position, blocks in cuts:
        heights = jax.random.uniform(jax.random.fold_in(jax.random.fold_in(stream_key, 6), position), (blocks,), jnp.float32, least / len(cuts), top_value / len(cuts))
        loudness = loudness * jnp.repeat(jnp.exp(heights), shape[position] // blocks).reshape((-1,) + (1,) * (len(shape) - 1 - position))
    return loudness


def scatter_about(stream_key, extent, deviation, most, pieces=(), kind=jnp.bfloat16):
    entries = jax.random.normal(stream_key, extent, jnp.float32) * deviation
    if len(pieces) > 0:
        entries = steps_of(stream_key, extent, pieces, -0.22, 0.18) * entries
    return jnp.clip(entries, min=-most, max=most).astype(kind)


def setup_inputs(seed: int = 0) -> dict:
    key_of = jax.random.split(jax.random.key(seed), 9)
    flow_speed = scatter_about(key_of[0], (3, 2, HARMONIC_NUMBER, GRIDPOINT_SUM), 1.0, 6.0, ((2, 16), (3, 32)))
    heat_state = scatter_about(key_of[1], (2, HARMONIC_NUMBER, GRIDPOINT_SUM), 1.0, 6.0, ((1, 16), (2, 32)), jnp.float32)
    planar_slope_matrices = scatter_about(key_of[2], (NE, 2, NODES, NODES), (2 * NODES) ** -0.5, 0.25, ((0, 32),))
    conduction_matrices = draw_conduction_matrices(jax.random.fold_in(key_of[8], 71), 0)
    adjacent_partners = draw_adjacent_partners(jax.random.fold_in(key_of[8], 71), 0)
    opposite_direction_flags = draw_opposite_direction_flags(jax.random.fold_in(key_of[8], 71), 0)
    interpatch_sides = draw_interpatch_sides(jax.random.fold_in(key_of[8], 71), 0)
    liquid_cells = draw_liquid_cells(jax.random.fold_in(key_of[8], 71), 0)
    return {"flow_speed": flow_speed, "heat_state": heat_state, "planar_slope_matrices": planar_slope_matrices, "conduction_matrices": conduction_matrices, "adjacent_partners": adjacent_partners, "opposite_direction_flags": opposite_direction_flags, "interpatch_sides": interpatch_sides, "liquid_cells": liquid_cells}


def make_table(modes_all, points):
    index_m = jnp.arange(modes_all, dtype=jnp.int32)[:, None]
    index_z = jnp.arange(points, dtype=jnp.int32)[None, :]
    phase = index_m * index_z % points
    angle = phase.astype(jnp.float32) * jnp.float32(2.0 * math.pi / points)
    values = jnp.stack([jnp.cos(angle), -jnp.sin(angle)]).astype(jnp.float32)
    return values.astype(jnp.bfloat16)

def traces_of(v5):
    edge = v5.shape[-1]
    return jnp.stack([v5[..., 0, :], v5[..., edge - 1, :], v5[..., :, 0], v5[..., :, edge - 1]], axis=-2)

def lift_faces(face_terms, edge):
    shape = face_terms.shape[:-2] + (edge, edge)
    out = jnp.zeros(shape, jnp.float32)
    out = out.at[..., 0, :].add(face_terms[..., 0, :])
    out = out.at[..., edge - 1, :].add(face_terms[..., 1, :])
    out = out.at[..., :, 0].add(face_terms[..., 2, :])
    out = out.at[..., :, edge - 1].add(face_terms[..., 3, :])
    return out

def apply_operator(v, stiff, adjacent_partners, opposite_direction_flags, interpatch_sides, harmonic_index):
    comps, modes_all, total = v.shape
    edge = EDGE
    v5 = v.reshape(comps, modes_all, NPATCHES, ELEMS, edge, edge)
    v4 = v.reshape(comps, modes_all, NPATCHES * ELEMS, NODES)
    local = jnp.einsum('ckeo,eno->cken', v4, stiff, precision=lax.Precision.HIGHEST)
    own = traces_of(v5).reshape(comps, modes_all, NPATCHES, ELEMS * 4, edge)
    bound = jnp.take_along_axis(own, interpatch_sides[None, None, :, :, None], axis=3)
    left = jnp.roll(bound[:, :, :, ROWS:], 1, axis=2)
    right = jnp.roll(bound[:, :, :, :ROWS], -1, axis=2)
    zero = jnp.zeros((comps, modes_all, NPATCHES, 1, edge), jnp.float32)
    pool = jnp.concatenate([own, left, right, zero], axis=3)
    index = adjacent_partners.reshape(NPATCHES, ELEMS * 4)
    partner = jnp.take_along_axis(pool, index[None, None, :, :, None], axis=3)
    flipped = opposite_direction_flags.reshape(NPATCHES, ELEMS * 4)[None, None, :, :, None] == 1
    partner = jnp.where(flipped, partner[..., ::-1], partner)
    jumps = 0.5 * (own - partner)
    jumps = jumps.reshape(comps, modes_all, NPATCHES, ELEMS, 4, edge)
    faces = lift_faces(jumps, edge).reshape(comps, modes_all, total)
    return (1.0 + harmonic_index * harmonic_index)[None, :, None] * v + local.reshape(comps, modes_all, total) + faces

def reference(flow_speed, heat_state, planar_slope_matrices, conduction_matrices, adjacent_partners, opposite_direction_flags, interpatch_sides, liquid_cells):
    ndev = ELEMS * NODES
    table = make_table(HARMONIC_NUMBER, ZP).astype(jnp.float32)
    scale = math.sqrt(2.0 / ZP)
    sampled_quantity = jnp.concatenate([flow_speed, heat_state.astype(jnp.bfloat16)[None]], axis=0)
    per = jnp.transpose(sampled_quantity.reshape(4, 2, HARMONIC_NUMBER, NPATCHES, ndev), (3, 0, 1, 2, 4))
    slots = jnp.arange(ndev, dtype=jnp.int32) // NODES
    fluid = (slots[None, :] < liquid_cells[:, None]).astype(jnp.float32)

    def one_patch(item):
        block, mask = item
        phys = jnp.einsum('fcmn,cmz->fnz', block.astype(jnp.float32), table) * scale
        flux = (phys[:3] * phys[3:4] * mask[None, :, None]).astype(jnp.bfloat16)
        back = jnp.einsum('fnz,cmz->fcmn', flux.astype(jnp.float32), table) * scale
        return back.astype(jnp.bfloat16)
    flux_hat = lax.map(one_patch, (per, fluid))
    flux_hat = jnp.transpose(flux_hat, (1, 2, 3, 0, 4)).reshape(3, 2, HARMONIC_NUMBER, GRIDPOINT_SUM)
    harmonic_index = jnp.arange(HARMONIC_NUMBER, dtype=jnp.int32).astype(jnp.float32) / HARMONIC_NUMBER
    sectional_slice = flux_hat[:2].astype(jnp.float32).reshape(2, 2, HARMONIC_NUMBER, NE, NODES)
    transport_heat_state = jnp.einsum('rsxfq,frhq->sxfh', sectional_slice, planar_slope_matrices.astype(jnp.float32)).reshape(2, HARMONIC_NUMBER, GRIDPOINT_SUM)
    lengthwise = flux_hat[2].astype(jnp.float32)
    transport_heat_state = transport_heat_state + jnp.stack([-harmonic_index[:, None] * lengthwise[1], harmonic_index[:, None] * lengthwise[0]])
    forcing_vector = heat_state - 0.5 * transport_heat_state
    stiff = conduction_matrices.astype(jnp.float32)
    theta, delta = (4.0, 3.0)
    sigma = theta / delta
    solution = jnp.zeros_like(forcing_vector)
    resid = forcing_vector
    walk = resid / theta
    rho = 1.0 / sigma
    for step in range(STEPS):
        image = apply_operator(walk, stiff, adjacent_partners, opposite_direction_flags, interpatch_sides, harmonic_index)
        solution = solution + walk
        resid = resid - image
        rho_new = 1.0 / (2.0 * sigma - rho)
        walk = rho_new * rho * walk + 2.0 * rho_new / delta * resid
        rho = rho_new
    return solution + walk
```

```python
import functools
import math

import jax
import jax.numpy as jnp
import numpy as np
from jax import lax
from jax.experimental import pallas as pl
from jax.experimental.pallas import tpu as pltpu
from jax.sharding import PartitionSpec as P

STEPS = 3
MESH = pl.DeviceIdType.MESH
F32 = jnp.float32
BF16 = jnp.bfloat16


def tables(modes, points, rows):
    half = points // 2
    z = np.arange(half + 1)
    m = np.arange(modes)
    phase = (z[:, None] * m[None, :]) % points
    angle = phase.astype(np.float32) * np.float32(2.0 * math.pi / points)
    out = np.zeros((2, rows, modes), np.float32)
    out[0, : half + 1] = np.cos(angle)
    out[1, : half + 1] = -np.sin(angle)
    out = out.astype(BF16)
    back = np.swapaxes(out, 1, 2).astype(np.float32)
    back[:, :, 0] *= 0.5
    back[:, :, half] *= 0.5
    return out, np.ascontiguousarray(back).astype(BF16)


def lift_table(elems, edge):
    nodes = edge * edge
    out = np.zeros((elems * 4 * edge, elems * nodes), np.float32)
    for e in range(elems):
        for i in range(edge):
            for face, node in enumerate((i, (edge - 1) * edge + i, i * edge, i * edge + edge - 1)):
                out[(e * 4 + face) * edge + i, e * nodes + node] = 1.0
    return out


def dot(a, b):
    return jnp.dot(a, b, preferred_element_type=F32)


def dot_nt(a, b):
    return lax.dot_general(a, b, (((1,), (1,)), ((), ())), preferred_element_type=F32)


def kernel(
    sizes,
    partners_ref,
    flags_ref,
    sides_ref,
    live_ref,
    flow_hbm,
    heat_hbm,
    slope_hbm,
    stiff_hbm,
    out_table_hbm,
    back_table_hbm,
    lift_hbm,
    lift_t_hbm,
    result_ref,
    flow,
    heat,
    slope,
    stiff,
    out_table,
    back_table,
    lift,
    lift_t,
    send1,
    recv1,
    flux_c,
    flux_s,
    send2,
    recv2,
    weights,
    dense,
    pick,
    halo_lift,
    halves,
    traces,
    halo,
    load_sem,
    own_sem,
    send1_sem,
    recv1_sem,
    send2_sem,
    recv2_sem,
    halo_send_sem,
    halo_recv_sem,
):
    parts, patches, mode_count, ndev, elems, edge, points = sizes
    modes = mode_count * parts
    nodes = edge * edge
    half = points // 2
    me = lax.axis_index("mode")
    patch = lax.axis_index("patch")
    left = lax.rem(patch + patches - 1, patches)
    right = lax.rem(patch + 1, patches)
    scale = math.sqrt(2.0 / points)

    loads = [
        pltpu.make_async_copy(src, dst, load_sem.at[i])
        for i, (src, dst) in enumerate(
            (
                (heat_hbm, heat),
                (flow_hbm, flow),
                (out_table_hbm, out_table),
                (back_table_hbm, back_table),
                (slope_hbm, slope),
                (stiff_hbm, stiff),
                (lift_hbm, lift),
                (lift_t_hbm, lift_t),
            )
        )
    ]
    for load in loads:
        load.start()

    barrier = pltpu.get_barrier_semaphore()
    for k in range(1, parts):
        pl.semaphore_signal(
            barrier, inc=1, device_id=(lax.rem(me + k, parts), patch), device_id_type=MESH
        )
    for side in (left, right):
        pl.semaphore_signal(barrier, inc=1, device_id=(me, side), device_id_type=MESH)

    low = lax.broadcasted_iota(jnp.int32, (mode_count, 128), 1) < 64

    def split(a, b):
        mask = lax.broadcasted_iota(jnp.int32, a.shape, 1) < 64
        return (
            jnp.where(mask, a, pltpu.roll(b, 64, 1)),
            jnp.where(mask, pltpu.roll(a, 64, 1), b),
        )

    loads[0].wait()
    loads[1].wait()
    barred = False
    for step in range(parts // 2):
        tile = lax.rem(me // 2 + step, parts // 2)
        cols = pl.ds(pl.multiple_of(tile * 128, 128), 128)
        for c in range(2):
            fields = [flow[f, c, :, cols].astype(F32) for f in range(3)]
            fields.append(heat[c, :, cols].astype(BF16).astype(F32))
            for pair in range(2):
                even, odd = split(fields[2 * pair], fields[2 * pair + 1])
                lanes = slice(128 * pair, 128 * pair + 128)
                send1[2 * tile, c, :, lanes] = even.astype(BF16)
                send1[2 * tile + 1, c, :, lanes] = odd.astype(BF16)
        if not barred:
            pl.semaphore_wait(barrier, parts + 1)
            barred = True
            own = pltpu.make_async_copy(
                send1.at[me], recv1.at[:, pl.ds(me * mode_count, mode_count), :], own_sem
            )
            own.start()
            other = lax.rem(me, 2)
            dests = [2 * tile + 1 - other]
        else:
            dests = [2 * tile, 2 * tile + 1]
        for dest in dests:
            pltpu.make_async_remote_copy(
                send1.at[dest],
                recv1.at[:, pl.ds(me * mode_count, mode_count), :],
                send1_sem.at[dest],
                recv1_sem.at[me],
                device_id=(dest, patch),
                device_id_type=MESH,
            ).start()

    for load in loads[2:]:
        load.wait()
    lane = lax.broadcasted_iota(jnp.int32, (1, 256), 1)
    group, offset = lane // edge, lane % edge
    source = jnp.full((1, 256), -1, jnp.int32)
    for e in range(elems):
        for face in range(4):
            there = jnp.where(flags_ref[e, face] == 1, edge - 1 - offset, offset)
            source = jnp.where(
                group == e * 4 + face, partners_ref[e, face] * edge + there, source
            )
    row = lax.broadcasted_iota(jnp.int32, (256, 256), 0)
    inner = jnp.where(row == source, 1.0, 0.0).astype(BF16)
    inner = dot(inner, lift[...]).astype(BF16)
    row = lax.broadcasted_iota(jnp.int32, (128, 256), 0)
    wanted = jnp.where(row < 2 * edge, 18 * edge + row, 16 * edge + row - 2 * edge)
    wanted = jnp.where(row < 4 * edge, wanted, -2)
    outer = jnp.where(wanted == source, -0.5, 0.0).astype(BF16)
    halo_lift[...] = dot(outer, lift[...]).astype(BF16)
    row = lax.broadcasted_iota(jnp.int32, (256, 128), 0)
    col = lax.broadcasted_iota(jnp.int32, (256, 128), 1)
    chosen = jnp.full((256, 128), -1, jnp.int32)
    for s in range(4):
        chosen = jnp.where(col // edge == s, sides_ref[0, s] * edge + col % edge, chosen)
    pick[...] = dot(lift_t[...], jnp.where(row == chosen, 1.0, 0.0).astype(BF16)).astype(BF16)
    for e in range(elems):
        for g in range(elems):
            rows = slice(g * nodes, g * nodes + nodes)
            cols = slice(e * nodes, e * nodes + nodes)
            block = -0.5 * dot(lift_t[rows, :], inner[:, cols])
            if g == e:
                block = block + stiff[e].astype(F32)
            dense[rows, cols] = block.astype(BF16)
    for e in range(elems):
        for q in range(2):
            lanes = slice(128 * q, 128 * q + 128)
            even, odd = split(slope[e, 0, :, lanes].astype(F32), slope[e, 1, :, lanes].astype(F32))
            weights[e, :, 256 * q : 256 * q + 128] = even.astype(BF16)
            weights[e, :, 256 * q + 128 : 256 * q + 256] = odd.astype(BF16)

    tail = half + 16
    flux_c[tail:, :] = jnp.zeros((flux_c.shape[0] - tail, 256), BF16)

    for k in range(1, parts):
        peer = lax.rem(me + k, parts)
        pltpu.make_async_remote_copy(
            send1.at[peer],
            recv1.at[:, pl.ds(peer * mode_count, mode_count), :],
            send1_sem.at[peer],
            recv1_sem.at[peer],
            device_id=(peer, patch),
            device_id_type=MESH,
        ).wait()
    own.wait()

    element = me // (parts // elems)
    wet = jnp.where(element < live_ref[0], scale * scale, 0.0).astype(F32)
    for first, count in ((0, 512), (512, 512), (1024, 512), (1536, 16)):
        rows = slice(first, first + count)
        even = dot(out_table[0, rows, :], recv1[0])
        odd = dot(out_table[1, rows, :], recv1[1])
        mask = lax.broadcasted_iota(jnp.int32, (count, 128), 1) < 64
        flux = []
        for field in (even + odd, even - odd):
            last = field[:, 128:]
            turned = pltpu.roll(last, 64, 1)
            warm = jnp.where(mask, turned, last) * wet
            flux.append((field[:, :128] * warm, last * turned * wet))
        for pair in range(2):
            lanes = slice(128 * pair, 128 * pair + 128)
            flux_c[rows, lanes] = (flux[0][pair] + flux[1][pair]).astype(BF16)
            if count > 16:
                flux_s[rows, lanes] = (flux[0][pair] - flux[1][pair]).astype(BF16)
    even = dot(back_table[0], flux_c[...]) * scale
    odd = dot(back_table[1, :, :half], flux_s[...]) * scale
    mask = lax.broadcasted_iota(jnp.int32, (modes, 128), 1) < 64
    send2[0] = even[:, :128].astype(BF16)
    send2[1] = odd[:, :128].astype(BF16)
    send2[2] = jnp.where(mask, even[:, 128:], odd[:, 128:]).astype(BF16)

    mine = pl.ds(pl.multiple_of(me * 128, 128), 128)
    own = pltpu.make_async_copy(
        send2.at[:, pl.ds(me * mode_count, mode_count), :], recv2.at[:, :, mine], own_sem
    )
    own.start()
    flights = []
    for k in range(1, parts):
        peer = lax.rem(me + k, parts)
        flights.append(
            pltpu.make_async_remote_copy(
                send2.at[:, pl.ds(peer * mode_count, mode_count), :],
                recv2.at[:, :, mine],
                send2_sem.at[k],
                recv2_sem.at[k],
                device_id=(peer, patch),
                device_id_type=MESH,
            )
        )
        flights[-1].start()
    for flight in flights:
        flight.wait()
    own.wait()

    wave = (lax.broadcasted_iota(jnp.int32, (mode_count, 1), 0) + me * mode_count).astype(F32)
    wave = wave / modes
    rhs = []
    moved = [
        dot_nt(recv2[0:2, :, 512 * e : 512 * e + 512].reshape(2 * mode_count, 512), weights[e])
        for e in range(elems)
    ]
    moved = jnp.concatenate(moved, axis=1)
    around = [[], []]
    for t in range(ndev // 128):
        even = recv2[2, :, 256 * t : 256 * t + 128].astype(F32)
        odd = recv2[2, :, 256 * t + 128 : 256 * t + 256].astype(F32)
        cosine, sine = split(even, odd)
        around[0].append(-wave * sine)
        around[1].append(wave * cosine)
    around = jnp.concatenate([jnp.concatenate(a, axis=1) for a in around], axis=0)
    rhs = heat[...].reshape(2 * mode_count, ndev) - 0.5 * (moved + around)

    wave2 = jnp.concatenate([wave, wave], axis=0)
    lane = lax.broadcasted_iota(jnp.int32, (1, ndev), 1)
    a, b = lane // edge % edge, lane % edge
    faces = sum(jnp.where(hit, 0.5, 0.0) for hit in (a == 0, a == edge - 1, b == 0, b == edge - 1))
    factor = (1.0 + wave2 * wave2) + faces
    rows2 = 2 * mode_count
    theta, delta = (4.0, 3.0)
    sigma = theta / delta
    total = jnp.zeros_like(rhs)
    resid = rhs
    walk = resid / theta
    rho = 1.0 / sigma
    right_lane = lax.broadcasted_iota(jnp.int32, (rows2, 128), 1) < 2 * edge
    for step in range(STEPS):
        high = walk.astype(BF16)
        halves[:rows2, :] = high
        halves[rows2:, :] = (walk - high.astype(F32)).astype(BF16)
        traces[step] = dot(high, pick[...]).astype(BF16)
        flights = []
        for side, dest in enumerate((right, left)):
            flights.append(
                pltpu.make_async_remote_copy(
                    traces.at[step],
                    halo.at[step, side],
                    halo_send_sem.at[step, side],
                    halo_recv_sem.at[step, side],
                    device_id=(me, dest),
                    device_id_type=MESH,
                )
            )
            flights[-1].start()
        local = dot(halves[...], dense[...])
        image = factor * walk + local[:rows2] + local[rows2:]
        for flight in flights:
            flight.wait()
        outside = jnp.where(right_lane, halo[step, 1].astype(F32), halo[step, 0].astype(F32)).astype(BF16)
        image = image + dot(outside, halo_lift[...])
        total = total + walk
        resid = resid - image
        rho_new = 1.0 / (2.0 * sigma - rho)
        walk = rho_new * rho * walk + 2.0 * rho_new / delta * resid
        rho = rho_new
    result_ref[...] = (total + walk).reshape(2, mode_count, ndev)


def per_device(
    flow_speed,
    heat_state,
    planar_slope_matrices,
    conduction_matrices,
    adjacent_partners,
    opposite_direction_flags,
    interpatch_sides,
    liquid_cells,
):
    parts = lax.axis_size("mode")
    patches = lax.axis_size("patch")
    _, _, mode_count, ndev = flow_speed.shape
    elems, nodes, _ = conduction_matrices.shape
    edge = math.isqrt(nodes)
    modes = mode_count * parts
    points = 3 * modes
    rows = points // 2 + 128
    out_table, back_table = tables(modes, points, rows)
    lift = lift_table(elems, edge)
    sizes = (parts, patches, mode_count, ndev, elems, edge, points)
    smem = pl.BlockSpec(memory_space=pltpu.SMEM)
    hbm = pl.BlockSpec(memory_space=pl.ANY)
    vmem = pl.BlockSpec(memory_space=pltpu.VMEM)
    big = (
        flow_speed,
        heat_state,
        planar_slope_matrices,
        conduction_matrices,
        jnp.asarray(out_table),
        jnp.asarray(back_table),
        jnp.asarray(lift.astype(BF16)),
        jnp.asarray(lift.T.astype(BF16)),
    )
    return pl.pallas_call(
        functools.partial(kernel, sizes),
        out_shape=jax.ShapeDtypeStruct(heat_state.shape, F32),
        in_specs=[smem] * 4 + [hbm] * 8,
        out_specs=vmem,
        scratch_shapes=[pltpu.VMEM(a.shape, a.dtype) for a in big]
        + [
            pltpu.VMEM((parts, 2, mode_count, 256), BF16),
            pltpu.VMEM((2, modes, 256), BF16),
            pltpu.VMEM((rows, 256), BF16),
            pltpu.VMEM((points // 2, 256), BF16),
            pltpu.VMEM((3, modes, 128), BF16),
            pltpu.VMEM((3, mode_count, parts * 128), BF16),
            pltpu.VMEM((elems, nodes, 2 * nodes), BF16),
            pltpu.VMEM((ndev, ndev), BF16),
            pltpu.VMEM((ndev, 128), BF16),
            pltpu.VMEM((128, ndev), BF16),
            pltpu.VMEM((4 * mode_count, ndev), BF16),
            pltpu.VMEM((STEPS, 2 * mode_count, 128), BF16),
            pltpu.VMEM((STEPS, 2, 2 * mode_count, 128), BF16),
            pltpu.SemaphoreType.DMA((8,)),
            pltpu.SemaphoreType.DMA,
            pltpu.SemaphoreType.DMA((parts,)),
            pltpu.SemaphoreType.DMA((parts,)),
            pltpu.SemaphoreType.DMA((parts,)),
            pltpu.SemaphoreType.DMA((parts,)),
            pltpu.SemaphoreType.DMA((STEPS, 2)),
            pltpu.SemaphoreType.DMA((STEPS, 2)),
        ],
        compiler_params=pltpu.CompilerParams(
            collective_id=0, has_side_effects=True, vmem_limit_bytes=56 << 20
        ),
    )(adjacent_partners, opposite_direction_flags, interpatch_sides, liquid_cells, *big)


def solution(mesh):
    placed = (
        P(None, None, "mode", "patch"),
        P(None, "mode", "patch"),
        P("patch", None, None, None),
        P("patch", None, None),
        P("patch", None),
        P("patch", None),
        P("patch", None),
        P("patch"),
    )
    return jax.shard_map(
        per_device, mesh=mesh, in_specs=placed, out_specs=P(None, "mode", "patch"), check_vma=False
    )
```

```python
import functools
import math

import jax
import jax.numpy as jnp
import numpy as np
from jax import lax
from jax.experimental import pallas as pl
from jax.experimental.pallas import tpu as pltpu
from jax.sharding import PartitionSpec as P

STEPS = 3
MESH = pl.DeviceIdType.MESH
F32 = jnp.float32
BF16 = jnp.bfloat16


def tables(modes, points, rows):
    half = points // 2
    z = np.arange(half + 1)
    m = np.arange(modes)
    phase = (z[:, None] * m[None, :]) % points
    angle = phase.astype(np.float32) * np.float32(2.0 * math.pi / points)
    out = np.zeros((2, rows, modes), np.float32)
    out[0, : half + 1] = np.cos(angle)
    out[1, : half + 1] = -np.sin(angle)
    out = out.astype(BF16)
    back = np.swapaxes(out, 1, 2).astype(np.float32)
    back[:, :, 0] *= 0.5
    back[:, :, half] *= 0.5
    return out, np.ascontiguousarray(back).astype(BF16)


def lift_table(elems, edge):
    nodes = edge * edge
    out = np.zeros((elems * 4 * edge, elems * nodes), np.float32)
    for e in range(elems):
        for i in range(edge):
            for face, node in enumerate((i, (edge - 1) * edge + i, i * edge, i * edge + edge - 1)):
                out[(e * 4 + face) * edge + i, e * nodes + node] = 1.0
    return out


def dot(a, b):
    return jnp.dot(a, b, preferred_element_type=F32)


def dot_nt(a, b):
    return lax.dot_general(a, b, (((1,), (1,)), ((), ())), preferred_element_type=F32)


def kernel(
    sizes,
    partners_ref,
    flags_ref,
    sides_ref,
    live_ref,
    flow_hbm,
    heat_hbm,
    slope_hbm,
    stiff_hbm,
    out_table_hbm,
    back_table_hbm,
    lift_hbm,
    lift_t_hbm,
    result_ref,
    flow,
    heat,
    slope,
    stiff,
    out_table,
    back_table,
    lift,
    lift_t,
    send1,
    recv1,
    flux_c,
    flux_s,
    send2,
    recv2,
    weights,
    dense,
    pick,
    spread,
    respond,
    respond_in,
    traces,
    halo,
    load_sem,
    own_sem,
    send1_sem,
    recv1_sem,
    send2_sem,
    recv2_sem,
    halo_send_sem,
    halo_recv_sem,
    respond_send_sem,
    respond_recv_sem,
):
    parts, patches, mode_count, ndev, elems, edge, points = sizes
    modes = mode_count * parts
    nodes = edge * edge
    half = points // 2
    me = lax.axis_index("mode")
    patch = lax.axis_index("patch")
    left = lax.rem(patch + patches - 1, patches)
    right = lax.rem(patch + 1, patches)
    scale = math.sqrt(2.0 / points)

    loads = [
        pltpu.make_async_copy(src, dst, load_sem.at[i])
        for i, (src, dst) in enumerate(
            (
                (heat_hbm, heat),
                (flow_hbm, flow),
                (out_table_hbm, out_table),
                (back_table_hbm, back_table),
                (slope_hbm, slope),
                (stiff_hbm, stiff),
                (lift_hbm, lift),
                (lift_t_hbm, lift_t),
            )
        )
    ]
    for load in loads:
        load.start()

    barrier = pltpu.get_barrier_semaphore()
    for k in range(1, parts):
        pl.semaphore_signal(
            barrier, inc=1, device_id=(lax.rem(me + k, parts), patch), device_id_type=MESH
        )
    for side in (left, right):
        pl.semaphore_signal(barrier, inc=1, device_id=(me, side), device_id_type=MESH)

    low = lax.broadcasted_iota(jnp.int32, (mode_count, 128), 1) < 64

    def split(a, b):
        mask = lax.broadcasted_iota(jnp.int32, a.shape, 1) < 64
        return (
            jnp.where(mask, a, pltpu.roll(b, 64, 1)),
            jnp.where(mask, pltpu.roll(a, 64, 1), b),
        )

    loads[0].wait()
    loads[1].wait()
    barred = False
    for step in range(parts // 2):
        tile = lax.rem(me // 2 + step, parts // 2)
        cols = pl.ds(pl.multiple_of(tile * 128, 128), 128)
        for c in range(2):
            fields = [flow[f, c, :, cols].astype(F32) for f in range(3)]
            fields.append(heat[c, :, cols].astype(BF16).astype(F32))
            for pair in range(2):
                even, odd = split(fields[2 * pair], fields[2 * pair + 1])
                lanes = slice(128 * pair, 128 * pair + 128)
                send1[2 * tile, c, :, lanes] = even.astype(BF16)
                send1[2 * tile + 1, c, :, lanes] = odd.astype(BF16)
        if not barred:
            pl.semaphore_wait(barrier, parts + 1)
            barred = True
            own = pltpu.make_async_copy(
                send1.at[me], recv1.at[:, pl.ds(me * mode_count, mode_count), :], own_sem
            )
            own.start()
            other = lax.rem(me, 2)
            dests = [2 * tile + 1 - other]
        else:
            dests = [2 * tile, 2 * tile + 1]
        for dest in dests:
            pltpu.make_async_remote_copy(
                send1.at[dest],
                recv1.at[:, pl.ds(me * mode_count, mode_count), :],
                send1_sem.at[dest],
                recv1_sem.at[me],
                device_id=(dest, patch),
                device_id_type=MESH,
            ).start()

    for load in loads[2:]:
        load.wait()
    lane = lax.broadcasted_iota(jnp.int32, (1, 256), 1)
    group, offset = lane // edge, lane % edge
    source = jnp.full((1, 256), -1, jnp.int32)
    for e in range(elems):
        for face in range(4):
            there = jnp.where(flags_ref[e, face] == 1, edge - 1 - offset, offset)
            source = jnp.where(
                group == e * 4 + face, partners_ref[e, face] * edge + there, source
            )
    row = lax.broadcasted_iota(jnp.int32, (256, 256), 0)
    inner = jnp.where(row == source, 1.0, 0.0).astype(BF16)
    inner = dot(inner, lift[...]).astype(BF16)
    row = lax.broadcasted_iota(jnp.int32, (128, 256), 0)
    wanted = jnp.where(row < 2 * edge, 18 * edge + row, 16 * edge + row - 2 * edge)
    wanted = jnp.where(row < 4 * edge, wanted, -2)
    outer = jnp.where(wanted == source, 0.5, 0.0).astype(BF16)
    row = lax.broadcasted_iota(jnp.int32, (256, 128), 0)
    col = lax.broadcasted_iota(jnp.int32, (256, 128), 1)
    chosen = jnp.full((256, 128), -1, jnp.int32)
    for s in range(4):
        chosen = jnp.where(col // edge == s, sides_ref[0, s] * edge + col % edge, chosen)
    chosen = jnp.where(row == chosen, 1.0, 0.0).astype(BF16)
    same = lax.broadcasted_iota(jnp.int32, (nodes, nodes), 0) == lax.broadcasted_iota(
        jnp.int32, (nodes, nodes), 1
    )
    lane_diag, row_diag = [], []
    for e in range(elems):
        for g in range(elems):
            rows = slice(g * nodes, g * nodes + nodes)
            cols = slice(e * nodes, e * nodes + nodes)
            block = -0.5 * dot(lift_t[rows, :], inner[:, cols])
            if g == e:
                full = stiff[e].astype(F32)
                diagonal = jnp.where(same, full, 0.0)
                lane_diag.append(jnp.sum(diagonal, axis=0, keepdims=True))
                row_diag.append(jnp.sum(diagonal, axis=1, keepdims=True))
                block = block + (full - diagonal)
            dense[rows, cols] = block.astype(BF16)

    def own_factor(axis):
        shape = (1, ndev) if axis else (ndev, 1)
        node = lax.broadcasted_iota(jnp.int32, shape, axis)
        a, b = node // edge % edge, node % edge
        hits = (a == 0, a == edge - 1, b == 0, b == edge - 1)
        return 1.0 + sum(jnp.where(hit, 0.5, 0.0) for hit in hits)

    factor = own_factor(1) + jnp.concatenate(lane_diag, axis=1)
    row_factor = own_factor(0) + jnp.concatenate(row_diag, axis=0)
    trace = dot(lift_t[...], chosen)
    pick[:, 0:128] = trace.astype(BF16)
    trace = trace * row_factor + dot(dense[...], pick[:, 0:128])
    pick[:, 128:256] = trace.astype(BF16)
    trace = trace * row_factor + dot(dense[...], pick[:, 128:256])
    pick[:, 256:384] = trace.astype(BF16)
    lifted = dot(outer, lift[...])
    spread[0:128, :] = lifted.astype(BF16)
    respond[0] = dot(spread[0:128, :], pick[:, 0:128]).astype(BF16)
    respond[1] = dot(spread[0:128, :], pick[:, 128:256]).astype(BF16)
    answers = []
    for side, dest in enumerate((right, left)):
        answers.append(
            pltpu.make_async_remote_copy(
                respond,
                respond_in.at[side],
                respond_send_sem.at[side],
                respond_recv_sem.at[side],
                device_id=(me, dest),
                device_id_type=MESH,
            )
        )
        answers[-1].start()
    lifted = lifted * factor + dot(spread[0:128, :], dense[...])
    spread[128:256, :] = lifted.astype(BF16)
    lifted = lifted * factor + dot(spread[128:256, :], dense[...])
    spread[256:384, :] = lifted.astype(BF16)
    for e in range(elems):
        for q in range(2):
            lanes = slice(128 * q, 128 * q + 128)
            even, odd = split(slope[e, 0, :, lanes].astype(F32), slope[e, 1, :, lanes].astype(F32))
            weights[e, :, 256 * q : 256 * q + 128] = even.astype(BF16)
            weights[e, :, 256 * q + 128 : 256 * q + 256] = odd.astype(BF16)

    tail = half + 16
    flux_c[tail:, :] = jnp.zeros((flux_c.shape[0] - tail, 256), BF16)

    for k in range(1, parts):
        peer = lax.rem(me + k, parts)
        pltpu.make_async_remote_copy(
            send1.at[peer],
            recv1.at[:, pl.ds(peer * mode_count, mode_count), :],
            send1_sem.at[peer],
            recv1_sem.at[peer],
            device_id=(peer, patch),
            device_id_type=MESH,
        ).wait()
    own.wait()

    element = me // (parts // elems)
    wet = jnp.where(element < live_ref[0], scale * scale, 0.0).astype(F32)
    for first, count in ((0, 512), (512, 512), (1024, 512), (1536, 16)):
        rows = slice(first, first + count)
        even = dot(out_table[0, rows, :], recv1[0])
        odd = dot(out_table[1, rows, :], recv1[1])
        mask = lax.broadcasted_iota(jnp.int32, (count, 128), 1) < 64
        flux = []
        for field in (even + odd, even - odd):
            last = field[:, 128:]
            turned = pltpu.roll(last, 64, 1)
            warm = jnp.where(mask, turned, last) * wet
            flux.append((field[:, :128] * warm, last * turned * wet))
        for pair in range(2):
            lanes = slice(128 * pair, 128 * pair + 128)
            flux_c[rows, lanes] = (flux[0][pair] + flux[1][pair]).astype(BF16)
            if count > 16:
                flux_s[rows, lanes] = (flux[0][pair] - flux[1][pair]).astype(BF16)
    even = dot(back_table[0], flux_c[...]) * scale
    odd = dot(back_table[1, :, :half], flux_s[...]) * scale
    mask = lax.broadcasted_iota(jnp.int32, (modes, 128), 1) < 64
    send2[0] = even[:, :128].astype(BF16)
    send2[1] = odd[:, :128].astype(BF16)
    send2[2] = jnp.where(mask, even[:, 128:], odd[:, 128:]).astype(BF16)

    mine = pl.ds(pl.multiple_of(me * 128, 128), 128)
    own = pltpu.make_async_copy(
        send2.at[:, pl.ds(me * mode_count, mode_count), :], recv2.at[:, :, mine], own_sem
    )
    own.start()
    flights = []
    for k in range(1, parts):
        peer = lax.rem(me + k, parts)
        flights.append(
            pltpu.make_async_remote_copy(
                send2.at[:, pl.ds(peer * mode_count, mode_count), :],
                recv2.at[:, :, mine],
                send2_sem.at[k],
                recv2_sem.at[k],
                device_id=(peer, patch),
                device_id_type=MESH,
            )
        )
        flights[-1].start()
    for flight in flights:
        flight.wait()
    own.wait()

    wave = (lax.broadcasted_iota(jnp.int32, (mode_count, 1), 0) + me * mode_count).astype(F32)
    wave = wave / modes
    rhs = []
    moved = [
        dot_nt(recv2[0:2, :, 512 * e : 512 * e + 512].reshape(2 * mode_count, 512), weights[e])
        for e in range(elems)
    ]
    moved = jnp.concatenate(moved, axis=1)
    around = [[], []]
    for t in range(ndev // 128):
        even = recv2[2, :, 256 * t : 256 * t + 128].astype(F32)
        odd = recv2[2, :, 256 * t + 128 : 256 * t + 256].astype(F32)
        cosine, sine = split(even, odd)
        around[0].append(-wave * sine)
        around[1].append(wave * cosine)
    around = jnp.concatenate([jnp.concatenate(a, axis=1) for a in around], axis=0)
    rhs = heat[...].reshape(2 * mode_count, ndev) - 0.5 * (moved + around)

    theta, delta = (4.0, 3.0)
    sigma = theta / delta
    rho = 1.0 / sigma
    keep, take = [], []
    for step in range(STEPS):
        rho_new = 1.0 / (2.0 * sigma - rho)
        keep.append(rho_new * rho)
        take.append(2.0 * rho_new / delta)
        rho = rho_new
    (a0, a1, a2), (b0, b1, b2) = keep, take
    wave2 = jnp.concatenate([wave, wave], axis=0)
    wave2 = wave2 * wave2
    powers = dot(rhs.astype(BF16), pick[...])
    p0, p1, p2 = powers[:, 0:128], powers[:, 128:256], powers[:, 256:384]
    once = wave2 * p0 + p1
    twice = wave2 * once + wave2 * p1 + p2
    t0 = p0 / theta
    r1 = p0 - once / theta
    t1 = a0 * t0 + b0 * r1
    t2 = a1 * t1 + b1 * (r1 - ((a0 / theta + b0) * once - (b0 / theta) * twice))
    traces[0] = t0.astype(BF16)
    traces[1] = t1.astype(BF16)
    traces[2] = t2.astype(BF16)
    flights = []
    for side, dest in enumerate((right, left)):
        flights.append(
            pltpu.make_async_remote_copy(
                traces,
                halo.at[side],
                halo_send_sem.at[side],
                halo_recv_sem.at[side],
                device_id=(me, dest),
                device_id_type=MESH,
            )
        )
        flights[-1].start()

    every = wave2 + factor
    total = jnp.zeros_like(rhs)
    resid = rhs
    walk = resid / theta
    for step in range(STEPS):
        image = every * walk + dot(walk.astype(BF16), dense[...])
        total = total + walk
        resid = resid - image
        walk = keep[step] * walk + take[step] * resid
    result_ref[...] = (total + walk).reshape(2, mode_count, ndev)

    for answer in answers:
        answer.wait()
    below = lax.broadcasted_iota(jnp.int32, (128, 128), 0) < 2 * edge
    reply0 = jnp.where(below, respond_in[0, 0].astype(F32), respond_in[1, 0].astype(F32)).astype(BF16)
    reply1 = jnp.where(below, respond_in[0, 1].astype(F32), respond_in[1, 1].astype(F32)).astype(BF16)
    back0 = dot(traces[0], reply0)
    back1 = dot(traces[1], reply0)
    back00 = dot(traces[0], reply1)
    around0 = dot(respond[0], reply0).astype(BF16)

    for flight in flights:
        flight.wait()
    mine = lax.broadcasted_iota(jnp.int32, (2 * mode_count, 128), 1) < 2 * edge
    s0, s1, s2 = [
        jnp.where(mine, halo[1, step].astype(F32), halo[0, step].astype(F32))
        for step in range(STEPS)
    ]
    back1 = back1 + b0 * dot(s0.astype(BF16), around0)
    s1 = s1 + b0 * back0
    first = 1.0 - b0 * wave2
    s2 = s2 + (a1 * b0 + b1 * first) * back0 + b1 * (back1 - b0 * back00)
    grown = first * s0 + s1
    alpha = a1 * b0 * s0 + b1 * grown
    beta = -b1 * b0 * s0
    y0 = b0 * s0 + (1.0 + a2) * alpha + b2 * (grown - wave2 * alpha + s2)
    y1 = (1.0 + a2) * beta + b2 * (-b0 * s0 - wave2 * beta - alpha)
    y2 = -b2 * beta
    y = jnp.concatenate([y0.astype(BF16), y1.astype(BF16), y2.astype(BF16)], axis=1)
    outside = dot(y, spread[...])
    result_ref[...] = result_ref[...] + outside.reshape(2, mode_count, ndev)


def per_device(
    flow_speed,
    heat_state,
    planar_slope_matrices,
    conduction_matrices,
    adjacent_partners,
    opposite_direction_flags,
    interpatch_sides,
    liquid_cells,
):
    parts = lax.axis_size("mode")
    patches = lax.axis_size("patch")
    _, _, mode_count, ndev = flow_speed.shape
    elems, nodes, _ = conduction_matrices.shape
    edge = math.isqrt(nodes)
    modes = mode_count * parts
    points = 3 * modes
    rows = points // 2 + 128
    out_table, back_table = tables(modes, points, rows)
    lift = lift_table(elems, edge)
    sizes = (parts, patches, mode_count, ndev, elems, edge, points)
    smem = pl.BlockSpec(memory_space=pltpu.SMEM)
    hbm = pl.BlockSpec(memory_space=pl.ANY)
    vmem = pl.BlockSpec(memory_space=pltpu.VMEM)
    big = (
        flow_speed,
        heat_state,
        planar_slope_matrices,
        conduction_matrices,
        jnp.asarray(out_table),
        jnp.asarray(back_table),
        jnp.asarray(lift.astype(BF16)),
        jnp.asarray(lift.T.astype(BF16)),
    )
    return pl.pallas_call(
        functools.partial(kernel, sizes),
        out_shape=jax.ShapeDtypeStruct(heat_state.shape, F32),
        in_specs=[smem] * 4 + [hbm] * 8,
        out_specs=vmem,
        scratch_shapes=[pltpu.VMEM(a.shape, a.dtype) for a in big]
        + [
            pltpu.VMEM((parts, 2, mode_count, 256), BF16),
            pltpu.VMEM((2, modes, 256), BF16),
            pltpu.VMEM((rows, 256), BF16),
            pltpu.VMEM((points // 2, 256), BF16),
            pltpu.VMEM((3, modes, 128), BF16),
            pltpu.VMEM((3, mode_count, parts * 128), BF16),
            pltpu.VMEM((elems, nodes, 2 * nodes), BF16),
            pltpu.VMEM((ndev, ndev), BF16),
            pltpu.VMEM((ndev, STEPS * 128), BF16),
            pltpu.VMEM((STEPS * 128, ndev), BF16),
            pltpu.VMEM((2, 128, 128), BF16),
            pltpu.VMEM((2, 2, 128, 128), BF16),
            pltpu.VMEM((STEPS, 2 * mode_count, 128), BF16),
            pltpu.VMEM((2, STEPS, 2 * mode_count, 128), BF16),
            pltpu.SemaphoreType.DMA((8,)),
            pltpu.SemaphoreType.DMA,
            pltpu.SemaphoreType.DMA((parts,)),
            pltpu.SemaphoreType.DMA((parts,)),
            pltpu.SemaphoreType.DMA((parts,)),
            pltpu.SemaphoreType.DMA((parts,)),
            pltpu.SemaphoreType.DMA((2,)),
            pltpu.SemaphoreType.DMA((2,)),
            pltpu.SemaphoreType.DMA((2,)),
            pltpu.SemaphoreType.DMA((2,)),
        ],
        compiler_params=pltpu.CompilerParams(
            collective_id=0, has_side_effects=True, vmem_limit_bytes=56 << 20
        ),
    )(adjacent_partners, opposite_direction_flags, interpatch_sides, liquid_cells, *big)


def solution(mesh):
    placed = (
        P(None, None, "mode", "patch"),
        P(None, "mode", "patch"),
        P("patch", None, None, None),
        P("patch", None, None),
        P("patch", None),
        P("patch", None),
        P("patch", None),
        P("patch"),
    )
    return jax.shard_map(
        per_device, mesh=mesh, in_specs=placed, out_specs=P(None, "mode", "patch"), check_vma=False
    )
```

```python
import functools
import math

import jax
import jax.numpy as jnp
import numpy as np
from jax import lax
from jax.experimental import pallas as pl
from jax.experimental.pallas import tpu as pltpu
from jax.sharding import PartitionSpec as P

STEPS = 3
ORDER = (2, 1, 3, 0)
MESH = pl.DeviceIdType.MESH
F32 = jnp.float32
BF16 = jnp.bfloat16


def tables(modes, points, rows):
    half = points // 2
    z = np.arange(half + 1)
    m = np.arange(modes)
    phase = (z[:, None] * m[None, :]) % points
    angle = phase.astype(np.float32) * np.float32(2.0 * math.pi / points)
    out = np.zeros((2, rows, modes), np.float32)
    out[0, : half + 1] = np.cos(angle)
    out[1, : half + 1] = -np.sin(angle)
    out = out.astype(BF16)
    back = np.swapaxes(out, 1, 2).astype(np.float32)
    back[:, :, 0] *= 0.5
    back[:, :, half] *= 0.5
    return out, np.ascontiguousarray(back).astype(BF16)


def lift_table(elems, edge):
    nodes = edge * edge
    out = np.zeros((elems * 4 * edge, elems * nodes), np.float32)
    for e in range(elems):
        for i in range(edge):
            for face, node in enumerate((i, (edge - 1) * edge + i, i * edge, i * edge + edge - 1)):
                out[(e * 4 + face) * edge + i, e * nodes + node] = 1.0
    return out


def dot(a, b):
    return jnp.dot(a, b, preferred_element_type=F32)


def dot_nt(a, b):
    return lax.dot_general(a, b, (((1,), (1,)), ((), ())), preferred_element_type=F32)


def kernel(
    sizes,
    live_ref,
    partners_hbm,
    flags_hbm,
    sides_hbm,
    flow_hbm,
    heat_hbm,
    slope_hbm,
    stiff_hbm,
    out_table_hbm,
    back_table_hbm,
    lift_hbm,
    lift_t_hbm,
    result_ref,
    partners_ref,
    flags_ref,
    sides_ref,
    flow,
    heat,
    slope,
    stiff,
    out_table,
    back_table,
    lift,
    lift_t,
    send1,
    recv1,
    phys,
    flux_c,
    flux_s,
    send2,
    recv2,
    weights,
    forcing,
    dense,
    pick,
    spread,
    respond,
    respond_in,
    traces,
    halo,
    load_sem,
    own_sem,
    send1_sem,
    recv1_sem,
    send2_sem,
    recv2_sem,
    halo_send_sem,
    halo_recv_sem,
    respond_send_sem,
    respond_recv_sem,
):
    parts, patches, mode_count, ndev, elems, edge, points = sizes
    modes = mode_count * parts
    nodes = edge * edge
    half = points // 2
    me = lax.axis_index("mode")
    patch = lax.axis_index("patch")
    left = lax.rem(patch + patches - 1, patches)
    right = lax.rem(patch + 1, patches)
    scale = math.sqrt(2.0 / points)

    loads = [
        pltpu.make_async_copy(src, dst, load_sem.at[i])
        for i, (src, dst) in enumerate(
            (
                (heat_hbm, heat),
                (flow_hbm, flow),
                (out_table_hbm, out_table),
                (back_table_hbm, back_table),
                (slope_hbm, slope),
                (stiff_hbm, stiff),
                (lift_hbm, lift),
                (lift_t_hbm, lift_t),
                (partners_hbm, partners_ref),
                (flags_hbm, flags_ref),
                (sides_hbm, sides_ref),
            )
        )
    ]
    for load in loads:
        load.start()

    barrier = pltpu.get_barrier_semaphore()
    for k in range(1, parts):
        pl.semaphore_signal(
            barrier, inc=1, device_id=(lax.rem(me + k, parts), patch), device_id_type=MESH
        )
    for side in (left, right):
        pl.semaphore_signal(barrier, inc=1, device_id=(me, side), device_id_type=MESH)

    def split(a, b):
        mask = lax.broadcasted_iota(jnp.int32, a.shape, 1) < 64
        return (
            jnp.where(mask, a, pltpu.roll(b, 64, 1)),
            jnp.where(mask, pltpu.roll(a, 64, 1), b),
        )

    loads[0].wait()
    loads[1].wait()
    ring = parts // elems
    home, place = me // ring, lax.rem(me, ring)

    def mates(quarter):
        return [quarter * ring + lax.rem(place + k, ring) for k in range(1, ring + 1)]

    my_rows = pl.ds(pl.multiple_of(me * mode_count, mode_count), mode_count)
    for turn in ORDER:
        quarter = lax.rem(home + turn, elems)
        for half_tile in range(2):
            tile = 2 * quarter + half_tile
            cols = pl.ds(pl.multiple_of(tile * 128, 128), 128)
            for c in range(2):
                fields = [flow[f, c, :, cols].astype(F32) for f in range(3)]
                fields.append(heat[c, :, cols].astype(BF16).astype(F32))
                for pair in range(2):
                    even, odd = split(fields[2 * pair], fields[2 * pair + 1])
                    lanes = slice(128 * pair, 128 * pair + 128)
                    send1[2 * tile, c, :, lanes] = even.astype(BF16)
                    send1[2 * tile + 1, c, :, lanes] = odd.astype(BF16)
        if turn == ORDER[0]:
            pl.semaphore_wait(barrier, parts + 1)
        for dest in mates(quarter)[: ring if turn else ring - 1]:
            pltpu.make_async_remote_copy(
                send1.at[dest],
                recv1.at[:, my_rows, :],
                send1_sem.at[dest],
                recv1_sem.at[me],
                device_id=(dest, patch),
                device_id_type=MESH,
            ).start()
    own = pltpu.make_async_copy(send1.at[me], recv1.at[:, my_rows, :], own_sem)
    own.start()

    for load in loads[2:]:
        load.wait()
    lane = lax.broadcasted_iota(jnp.int32, (1, 256), 1)
    group, offset = lane // edge, lane % edge
    source = jnp.full((1, 256), -1, jnp.int32)
    for e in range(elems):
        for face in range(4):
            there = jnp.where(flags_ref[e, face] == 1, edge - 1 - offset, offset)
            source = jnp.where(
                group == e * 4 + face, partners_ref[e, face] * edge + there, source
            )
    row = lax.broadcasted_iota(jnp.int32, (256, 256), 0)
    inner = jnp.where(row == source, 1.0, 0.0).astype(BF16)
    inner = dot(inner, lift[...]).astype(BF16)
    row = lax.broadcasted_iota(jnp.int32, (128, 256), 0)
    wanted = jnp.where(row < 2 * edge, 18 * edge + row, 16 * edge + row - 2 * edge)
    wanted = jnp.where(row < 4 * edge, wanted, -2)
    outer = jnp.where(wanted == source, 0.5, 0.0).astype(BF16)
    row = lax.broadcasted_iota(jnp.int32, (256, 128), 0)
    col = lax.broadcasted_iota(jnp.int32, (256, 128), 1)
    chosen = jnp.full((256, 128), -1, jnp.int32)
    for s in range(4):
        chosen = jnp.where(col // edge == s, sides_ref[0, s] * edge + col % edge, chosen)
    chosen = jnp.where(row == chosen, 1.0, 0.0).astype(BF16)
    same = lax.broadcasted_iota(jnp.int32, (nodes, nodes), 0) == lax.broadcasted_iota(
        jnp.int32, (nodes, nodes), 1
    )
    lane_diag, row_diag = [], []
    for e in range(elems):
        for g in range(elems):
            rows = slice(g * nodes, g * nodes + nodes)
            cols = slice(e * nodes, e * nodes + nodes)
            block = -0.5 * dot(lift_t[rows, :], inner[:, cols])
            if g == e:
                full = stiff[e].astype(F32)
                diagonal = jnp.where(same, full, 0.0)
                lane_diag.append(jnp.sum(diagonal, axis=0, keepdims=True))
                row_diag.append(jnp.sum(diagonal, axis=1, keepdims=True))
                block = block + (full - diagonal)
            dense[rows, cols] = block.astype(BF16)

    def own_factor(axis):
        shape = (1, ndev) if axis else (ndev, 1)
        node = lax.broadcasted_iota(jnp.int32, shape, axis)
        a, b = node // edge % edge, node % edge
        hits = (a == 0, a == edge - 1, b == 0, b == edge - 1)
        return 1.0 + sum(jnp.where(hit, 0.5, 0.0) for hit in hits)

    factor = own_factor(1) + jnp.concatenate(lane_diag, axis=1)
    row_factor = own_factor(0) + jnp.concatenate(row_diag, axis=0)
    trace = dot(lift_t[...], chosen)
    pick[:, 0:128] = trace.astype(BF16)
    trace = trace * row_factor + dot(dense[...], pick[:, 0:128])
    pick[:, 128:256] = trace.astype(BF16)
    trace = trace * row_factor + dot(dense[...], pick[:, 128:256])
    pick[:, 256:384] = trace.astype(BF16)
    lifted = dot(outer, lift[...])
    spread[0:128, :] = lifted.astype(BF16)
    respond[0] = dot(spread[0:128, :], pick[:, 0:128]).astype(BF16)
    respond[1] = dot(spread[0:128, :], pick[:, 128:256]).astype(BF16)
    answers = []
    for side, dest in enumerate((right, left)):
        answers.append(
            pltpu.make_async_remote_copy(
                respond,
                respond_in.at[side],
                respond_send_sem.at[side],
                respond_recv_sem.at[side],
                device_id=(me, dest),
                device_id_type=MESH,
            )
        )
        answers[-1].start()
    lifted = lifted * factor + dot(spread[0:128, :], dense[...])
    spread[128:256, :] = lifted.astype(BF16)
    lifted = lifted * factor + dot(spread[128:256, :], dense[...])
    spread[256:384, :] = lifted.astype(BF16)
    for e in range(elems):
        for q in range(2):
            lanes = slice(128 * q, 128 * q + 128)
            even, odd = split(slope[e, 0, :, lanes].astype(F32), slope[e, 1, :, lanes].astype(F32))
            weights[e, :, 256 * q : 256 * q + 128] = even.astype(BF16)
            weights[e, :, 256 * q + 128 : 256 * q + 256] = odd.astype(BF16)

    tail = half + 16
    flux_c[tail:, :] = jnp.zeros((flux_c.shape[0] - tail, 256), BF16)

    def flight1(peer):
        rows = pl.ds(pl.multiple_of(peer * mode_count, mode_count), mode_count)
        return pltpu.make_async_remote_copy(
            send1.at[peer],
            recv1.at[:, rows, :],
            send1_sem.at[peer],
            recv1_sem.at[peer],
            device_id=(peer, patch),
            device_id_type=MESH,
        )

    wet = jnp.where(home < live_ref[0, 0], scale * scale, 0.0).astype(F32)
    span = ring * mode_count
    for turn in ORDER:
        quarter = lax.rem(home + elems - turn, elems)
        for source in mates(quarter)[: ring if turn else ring - 1]:
            flight1(source).wait_recv()
        if turn == 0:
            own.wait()
        depth = pl.ds(pl.multiple_of(quarter * span, span), span)
        for first, count in ((0, 512), (512, 512), (1024, 512), (1536, 16)):
            rows = slice(first, first + count)
            even = dot(out_table[0, rows, depth], recv1[0, depth, :])
            odd = dot(out_table[1, rows, depth], recv1[1, depth, :])
            if turn != ORDER[0]:
                even = even + phys[0, rows, :]
                odd = odd + phys[1, rows, :]
            if turn != ORDER[-1]:
                phys[0, rows, :] = even
                phys[1, rows, :] = odd
                continue
            mask = lax.broadcasted_iota(jnp.int32, (count, 128), 1) < 64
            flux = []
            for field in (even + odd, even - odd):
                last = field[:, 128:]
                turned = pltpu.roll(last, 64, 1)
                warm = jnp.where(mask, turned, last) * wet
                flux.append((field[:, :128] * warm, last * turned * wet))
            for pair in range(2):
                lanes = slice(128 * pair, 128 * pair + 128)
                flux_c[rows, lanes] = (flux[0][pair] + flux[1][pair]).astype(BF16)
                if count > 16:
                    flux_s[rows, lanes] = (flux[0][pair] - flux[1][pair]).astype(BF16)

    my_lanes = pl.ds(pl.multiple_of(me * 128, 128), 128)

    def flight2(peer, incoming):
        rows = pl.ds(pl.multiple_of(peer * mode_count, mode_count), mode_count)
        return pltpu.make_async_remote_copy(
            send2.at[:, rows, :],
            recv2.at[:, :, my_lanes],
            send2_sem.at[peer],
            recv2_sem.at[incoming],
            device_id=(peer, patch),
            device_id_type=MESH,
        )

    mask = lax.broadcasted_iota(jnp.int32, (span, 128), 1) < 64
    for turn in ORDER:
        quarter = lax.rem(home + turn, elems)
        rows = pl.ds(pl.multiple_of(quarter * span, span), span)
        even = dot(back_table[0, rows, :], flux_c[...]) * scale
        odd = dot(back_table[1, rows, :half], flux_s[...]) * scale
        send2[0, rows, :] = even[:, :128].astype(BF16)
        send2[1, rows, :] = odd[:, :128].astype(BF16)
        send2[2, rows, :] = jnp.where(mask, even[:, 128:], odd[:, 128:]).astype(BF16)
        for dest in mates(quarter)[: ring if turn else ring - 1]:
            flight2(dest, me).start()
    own = pltpu.make_async_copy(send2.at[:, my_rows, :], recv2.at[:, :, my_lanes], own_sem)
    own.start()
    for k in range(1, parts):
        flight1(lax.rem(me + k, parts)).wait_send()

    wave = (lax.broadcasted_iota(jnp.int32, (mode_count, 1), 0) + me * mode_count).astype(F32)
    wave = wave / modes
    powers = jnp.zeros((2 * mode_count, STEPS * 128), F32)
    for turn in ORDER:
        quarter = lax.rem(home + elems - turn, elems)
        for source in mates(quarter)[: ring if turn else ring - 1]:
            flight2(source, source).wait_recv()
        if turn == 0:
            own.wait()
        depth = pl.ds(pl.multiple_of(quarter * 2 * nodes, 2 * nodes), 2 * nodes)
        moved = dot_nt(
            recv2[0:2, :, depth].reshape(2 * mode_count, 2 * nodes), weights[quarter]
        )
        around = [[], []]
        for t in range(2):
            first = quarter * 2 * nodes + 256 * t
            even = recv2[2, :, pl.ds(pl.multiple_of(first, 128), 128)].astype(F32)
            odd = recv2[2, :, pl.ds(pl.multiple_of(first + 128, 128), 128)].astype(F32)
            cosine, sine = split(even, odd)
            around[0].append(-wave * sine)
            around[1].append(wave * cosine)
        around = jnp.concatenate([jnp.concatenate(a, axis=1) for a in around], axis=0)
        lanes = pl.ds(pl.multiple_of(quarter * nodes, nodes), nodes)
        part = heat[:, :, lanes].reshape(2 * mode_count, nodes) - 0.5 * (moved + around)
        forcing[:, lanes] = part
        powers = powers + dot(part.astype(BF16), pick[lanes, :])

    theta, delta = (4.0, 3.0)
    sigma = theta / delta
    rho = 1.0 / sigma
    keep, take = [], []
    for step in range(STEPS):
        rho_new = 1.0 / (2.0 * sigma - rho)
        keep.append(rho_new * rho)
        take.append(2.0 * rho_new / delta)
        rho = rho_new
    (a0, a1, a2), (b0, b1, b2) = keep, take
    wave2 = jnp.concatenate([wave, wave], axis=0)
    wave2 = wave2 * wave2
    p0, p1, p2 = powers[:, 0:128], powers[:, 128:256], powers[:, 256:384]
    once = wave2 * p0 + p1
    twice = wave2 * once + wave2 * p1 + p2
    t0 = p0 / theta
    r1 = p0 - once / theta
    t1 = a0 * t0 + b0 * r1
    t2 = a1 * t1 + b1 * (r1 - ((a0 / theta + b0) * once - (b0 / theta) * twice))
    traces[0] = t0.astype(BF16)
    traces[1] = t1.astype(BF16)
    traces[2] = t2.astype(BF16)
    flights = []
    for side, dest in enumerate((right, left)):
        flights.append(
            pltpu.make_async_remote_copy(
                traces,
                halo.at[side],
                halo_send_sem.at[side],
                halo_recv_sem.at[side],
                device_id=(me, dest),
                device_id_type=MESH,
            )
        )
        flights[-1].start()

    rhs = forcing[...]
    every = wave2 + factor
    total = jnp.zeros_like(rhs)
    resid = rhs
    walk = resid / theta
    for step in range(STEPS):
        image = every * walk + dot(walk.astype(BF16), dense[...])
        total = total + walk
        resid = resid - image
        walk = keep[step] * walk + take[step] * resid
    result_ref[...] = (total + walk).reshape(2, mode_count, ndev)

    for answer in answers:
        answer.wait()
    below = lax.broadcasted_iota(jnp.int32, (128, 128), 0) < 2 * edge
    reply0 = jnp.where(below, respond_in[0, 0].astype(F32), respond_in[1, 0].astype(F32)).astype(BF16)
    reply1 = jnp.where(below, respond_in[0, 1].astype(F32), respond_in[1, 1].astype(F32)).astype(BF16)
    back0 = dot(traces[0], reply0)
    back1 = dot(traces[1], reply0)
    back00 = dot(traces[0], reply1)
    around0 = dot(respond[0], reply0).astype(BF16)

    for k in range(1, parts):
        peer = lax.rem(me + k, parts)
        flight2(peer, peer).wait_send()
    for flight in flights:
        flight.wait()
    mine = lax.broadcasted_iota(jnp.int32, (2 * mode_count, 128), 1) < 2 * edge
    s0, s1, s2 = [
        jnp.where(mine, halo[1, step].astype(F32), halo[0, step].astype(F32))
        for step in range(STEPS)
    ]
    back1 = back1 + b0 * dot(s0.astype(BF16), around0)
    s1 = s1 + b0 * back0
    first = 1.0 - b0 * wave2
    s2 = s2 + (a1 * b0 + b1 * first) * back0 + b1 * (back1 - b0 * back00)
    grown = first * s0 + s1
    alpha = a1 * b0 * s0 + b1 * grown
    beta = -b1 * b0 * s0
    y0 = b0 * s0 + (1.0 + a2) * alpha + b2 * (grown - wave2 * alpha + s2)
    y1 = (1.0 + a2) * beta + b2 * (-b0 * s0 - wave2 * beta - alpha)
    y2 = -b2 * beta
    y = jnp.concatenate([y0.astype(BF16), y1.astype(BF16), y2.astype(BF16)], axis=1)
    outside = dot(y, spread[...])
    result_ref[...] = result_ref[...] + outside.reshape(2, mode_count, ndev)


def hand_over(solved_ref, result_ref, sem):
    copy = pltpu.make_async_copy(solved_ref, result_ref, sem)
    copy.start()
    copy.wait()


def per_device(
    flow_speed,
    heat_state,
    planar_slope_matrices,
    conduction_matrices,
    adjacent_partners,
    opposite_direction_flags,
    interpatch_sides,
    liquid_cells,
):
    parts = lax.axis_size("mode")
    patches = lax.axis_size("patch")
    _, _, mode_count, ndev = flow_speed.shape
    elems, nodes, _ = conduction_matrices.shape
    edge = math.isqrt(nodes)
    modes = mode_count * parts
    points = 3 * modes
    rows = points // 2 + 128
    out_table, back_table = tables(modes, points, rows)
    lift = lift_table(elems, edge)
    sizes = (parts, patches, mode_count, ndev, elems, edge, points)
    hbm = pl.BlockSpec(memory_space=pltpu.HBM)
    vmem = pl.BlockSpec(memory_space=pltpu.VMEM)
    small = (adjacent_partners, opposite_direction_flags, interpatch_sides)
    big = (
        flow_speed,
        heat_state,
        planar_slope_matrices,
        conduction_matrices,
        jnp.asarray(out_table),
        jnp.asarray(back_table),
        jnp.asarray(lift.astype(BF16)),
        jnp.asarray(lift.T.astype(BF16)),
    )
    solved = pl.pallas_call(
        functools.partial(kernel, sizes),
        out_shape=pltpu.VMEM(heat_state.shape, F32),
        in_specs=[pl.BlockSpec(memory_space=pltpu.SMEM)] + [hbm] * 11,
        out_specs=vmem,
        scratch_shapes=[pltpu.SMEM(a.shape, a.dtype) for a in small]
        + [pltpu.VMEM(a.shape, a.dtype) for a in big]
        + [
            pltpu.VMEM((parts, 2, mode_count, 256), BF16),
            pltpu.VMEM((2, modes, 256), BF16),
            pltpu.VMEM((2, points // 2 + 16, 256), F32),
            pltpu.VMEM((rows, 256), BF16),
            pltpu.VMEM((points // 2, 256), BF16),
            pltpu.VMEM((3, modes, 128), BF16),
            pltpu.VMEM((3, mode_count, parts * 128), BF16),
            pltpu.VMEM((elems, nodes, 2 * nodes), BF16),
            pltpu.VMEM((2 * mode_count, ndev), F32),
            pltpu.VMEM((ndev, ndev), BF16),
            pltpu.VMEM((ndev, STEPS * 128), BF16),
            pltpu.VMEM((STEPS * 128, ndev), BF16),
            pltpu.VMEM((2, 128, 128), BF16),
            pltpu.VMEM((2, 2, 128, 128), BF16),
            pltpu.VMEM((STEPS, 2 * mode_count, 128), BF16),
            pltpu.VMEM((2, STEPS, 2 * mode_count, 128), BF16),
            pltpu.SemaphoreType.DMA((11,)),
            pltpu.SemaphoreType.DMA,
            pltpu.SemaphoreType.DMA((parts,)),
            pltpu.SemaphoreType.DMA((parts,)),
            pltpu.SemaphoreType.DMA((parts,)),
            pltpu.SemaphoreType.DMA((parts,)),
            pltpu.SemaphoreType.DMA((2,)),
            pltpu.SemaphoreType.DMA((2,)),
            pltpu.SemaphoreType.DMA((2,)),
            pltpu.SemaphoreType.DMA((2,)),
        ],
        compiler_params=pltpu.CompilerParams(
            collective_id=0, has_side_effects=True, vmem_limit_bytes=52 << 20
        ),
    )(
        liquid_cells.reshape(1, 1),
        *[pltpu.with_memory_space_constraint(a, pltpu.HBM) for a in small + big],
    )
    return pl.pallas_call(
        hand_over,
        out_shape=jax.ShapeDtypeStruct(heat_state.shape, F32),
        in_specs=[vmem],
        out_specs=hbm,
        scratch_shapes=[pltpu.SemaphoreType.DMA],
        compiler_params=pltpu.CompilerParams(vmem_limit_bytes=4 << 20),
    )(solved)


def solution(mesh):
    placed = (
        P(None, None, "mode", "patch"),
        P(None, "mode", "patch"),
        P("patch", None, None, None),
        P("patch", None, None),
        P("patch", None),
        P("patch", None),
        P("patch", None),
        P("patch"),
    )
    return jax.shard_map(
        per_device, mesh=mesh, in_specs=placed, out_specs=P(None, "mode", "patch"), check_vma=False
    )
```

```python
import functools
import math

import jax
import jax.numpy as jnp
import numpy as np
from jax import lax
from jax.experimental import pallas as pl
from jax.experimental.pallas import tpu as pltpu
from jax.sharding import PartitionSpec as P

STEPS = 3
ORDER = (2, 1, 3, 0)
BACK_ORDER = (1, 3, 2, 0)
MESH = pl.DeviceIdType.MESH
F32 = jnp.float32
BF16 = jnp.bfloat16


def tables(modes, points, rows):
    half = points // 2
    z = np.arange(half + 1)
    m = np.arange(modes)
    phase = (z[:, None] * m[None, :]) % points
    angle = phase.astype(np.float32) * np.float32(2.0 * math.pi / points)
    out = np.zeros((2, rows, modes), np.float32)
    out[0, : half + 1] = np.cos(angle)
    out[1, : half + 1] = -np.sin(angle)
    out = out.astype(BF16)
    back = np.swapaxes(out, 1, 2).astype(np.float32)
    back[:, :, 0] *= 0.5
    back[:, :, half] *= 0.5
    return out, np.ascontiguousarray(back).astype(BF16)


def lift_table(elems, edge):
    nodes = edge * edge
    out = np.zeros((elems * 4 * edge, elems * nodes), np.float32)
    for e in range(elems):
        for i in range(edge):
            for face, node in enumerate((i, (edge - 1) * edge + i, i * edge, i * edge + edge - 1)):
                out[(e * 4 + face) * edge + i, e * nodes + node] = 1.0
    return out


def dot(a, b):
    return jnp.dot(a, b, preferred_element_type=F32)


def dot_nt(a, b):
    return lax.dot_general(a, b, (((1,), (1,)), ((), ())), preferred_element_type=F32)


def kernel(
    sizes,
    live_ref,
    partners_hbm,
    flags_hbm,
    sides_hbm,
    flow_hbm,
    heat_hbm,
    slope_hbm,
    stiff_hbm,
    out_table_hbm,
    back_table_hbm,
    lift_hbm,
    lift_t_hbm,
    result_ref,
    partners_ref,
    flags_ref,
    sides_ref,
    flow,
    heat,
    slope,
    stiff,
    out_table,
    back_table,
    lift,
    lift_t,
    send1,
    recv1,
    phys,
    warm,
    flux_c,
    flux_s,
    send2,
    recv2,
    weights,
    forcing,
    applied,
    dense,
    pick,
    spread,
    respond,
    respond_in,
    traces,
    halo,
    load_sem,
    own_sem,
    send1_sem,
    recv1_sem,
    send2_sem,
    recv2_sem,
    halo_send_sem,
    halo_recv_sem,
    respond_send_sem,
    respond_recv_sem,
):
    parts, patches, mode_count, ndev, elems, edge, points = sizes
    modes = mode_count * parts
    nodes = edge * edge
    half = points // 2
    me = lax.axis_index("mode")
    patch = lax.axis_index("patch")
    left = lax.rem(patch + patches - 1, patches)
    right = lax.rem(patch + 1, patches)
    scale = math.sqrt(2.0 / points)

    loads = [
        pltpu.make_async_copy(src, dst, load_sem.at[i])
        for i, (src, dst) in enumerate(
            (
                (heat_hbm, heat),
                (flow_hbm, flow),
                (out_table_hbm, out_table),
                (back_table_hbm, back_table),
                (slope_hbm, slope),
                (stiff_hbm, stiff),
                (lift_hbm, lift),
                (lift_t_hbm, lift_t),
                (partners_hbm, partners_ref),
                (flags_hbm, flags_ref),
                (sides_hbm, sides_ref),
            )
        )
    ]
    for load in loads[:2]:
        load.start()

    barrier = pltpu.get_barrier_semaphore()
    for k in range(1, parts):
        pl.semaphore_signal(
            barrier, inc=1, device_id=(lax.rem(me + k, parts), patch), device_id_type=MESH
        )
    for side in (left, right):
        pl.semaphore_signal(barrier, inc=1, device_id=(me, side), device_id_type=MESH)

    def split(a, b):
        mask = lax.broadcasted_iota(jnp.int32, a.shape, 1) < 64
        return (
            jnp.where(mask, a, pltpu.roll(b, 64, 1)),
            jnp.where(mask, pltpu.roll(a, 64, 1), b),
        )

    loads[0].wait()
    loads[1].wait()
    for load in loads[2:]:
        load.start()
    ring = parts // elems
    home, place = me // ring, lax.rem(me, ring)

    def mates(quarter):
        return [quarter * ring + lax.rem(place + k, ring) for k in range(1, ring + 1)]

    my_rows = pl.ds(pl.multiple_of(me * mode_count, mode_count), mode_count)
    owns = []
    for pair in (1, 0):
        lanes = slice(128 * pair, 128 * pair + 128)
        for turn in ORDER:
            quarter = lax.rem(home + turn, elems)
            for half_tile in range(2):
                tile = 2 * quarter + half_tile
                cols = pl.ds(pl.multiple_of(tile * 128, 128), 128)
                for c in range(2):
                    first = flow[2 * pair, c, :, cols].astype(F32)
                    if pair:
                        second = heat[c, :, cols].astype(BF16).astype(F32)
                    else:
                        second = flow[1, c, :, cols].astype(F32)
                    even, odd = split(first, second)
                    send1[2 * tile, pair, c] = even.astype(BF16)
                    send1[2 * tile + 1, pair, c] = odd.astype(BF16)
            if pair and turn == ORDER[0]:
                pl.semaphore_wait(barrier, parts + 1)
            for dest in mates(quarter)[: ring if turn else ring - 1]:
                pltpu.make_async_remote_copy(
                    send1.at[dest, pair],
                    recv1.at[pair, :, my_rows, :],
                    send1_sem.at[pair, dest],
                    recv1_sem.at[pair, me],
                    device_id=(dest, patch),
                    device_id_type=MESH,
                ).start()
        own = pltpu.make_async_copy(
            send1.at[me, pair], recv1.at[pair, :, my_rows, :], own_sem.at[pair]
        )
        own.start()
        owns.insert(0, own)

    for load in loads[2:]:
        load.wait()
    lane = lax.broadcasted_iota(jnp.int32, (1, 256), 1)
    group, offset = lane // edge, lane % edge
    source = jnp.full((1, 256), -1, jnp.int32)
    for e in range(elems):
        for face in range(4):
            there = jnp.where(flags_ref[e, face] == 1, edge - 1 - offset, offset)
            source = jnp.where(
                group == e * 4 + face, partners_ref[e, face] * edge + there, source
            )
    row = lax.broadcasted_iota(jnp.int32, (256, 256), 0)
    inner = jnp.where(row == source, 1.0, 0.0).astype(BF16)
    inner = dot(inner, lift[...]).astype(BF16)
    row = lax.broadcasted_iota(jnp.int32, (128, 256), 0)
    wanted = jnp.where(row < 2 * edge, 18 * edge + row, 16 * edge + row - 2 * edge)
    wanted = jnp.where(row < 4 * edge, wanted, -2)
    outer = jnp.where(wanted == source, 0.5, 0.0).astype(BF16)
    row = lax.broadcasted_iota(jnp.int32, (256, 128), 0)
    col = lax.broadcasted_iota(jnp.int32, (256, 128), 1)
    chosen = jnp.full((256, 128), -1, jnp.int32)
    for s in range(4):
        chosen = jnp.where(col // edge == s, sides_ref[0, s] * edge + col % edge, chosen)
    chosen = jnp.where(row == chosen, 1.0, 0.0).astype(BF16)
    same = lax.broadcasted_iota(jnp.int32, (nodes, nodes), 0) == lax.broadcasted_iota(
        jnp.int32, (nodes, nodes), 1
    )
    lane_diag, row_diag = [], []
    for e in range(elems):
        for g in range(elems):
            rows = slice(g * nodes, g * nodes + nodes)
            cols = slice(e * nodes, e * nodes + nodes)
            block = -0.5 * dot(lift_t[rows, :], inner[:, cols])
            if g == e:
                full = stiff[e].astype(F32)
                diagonal = jnp.where(same, full, 0.0)
                lane_diag.append(jnp.sum(diagonal, axis=0, keepdims=True))
                row_diag.append(jnp.sum(diagonal, axis=1, keepdims=True))
                block = block + (full - diagonal)
            dense[rows, cols] = block.astype(BF16)

    def own_factor(axis):
        shape = (1, ndev) if axis else (ndev, 1)
        node = lax.broadcasted_iota(jnp.int32, shape, axis)
        a, b = node // edge % edge, node % edge
        hits = (a == 0, a == edge - 1, b == 0, b == edge - 1)
        return 1.0 + sum(jnp.where(hit, 0.5, 0.0) for hit in hits)

    factor = own_factor(1) + jnp.concatenate(lane_diag, axis=1)
    row_factor = own_factor(0) + jnp.concatenate(row_diag, axis=0)
    trace = dot(lift_t[...], chosen)
    pick[:, 0:128] = trace.astype(BF16)
    trace = trace * row_factor + dot(dense[...], pick[:, 0:128])
    pick[:, 128:256] = trace.astype(BF16)
    trace = trace * row_factor + dot(dense[...], pick[:, 128:256])
    pick[:, 256:384] = trace.astype(BF16)
    lifted = dot(outer, lift[...])
    spread[0:128, :] = lifted.astype(BF16)
    respond[0] = dot(spread[0:128, :], pick[:, 0:128]).astype(BF16)
    respond[1] = dot(spread[0:128, :], pick[:, 128:256]).astype(BF16)
    answers = []
    for side, dest in enumerate((right, left)):
        answers.append(
            pltpu.make_async_remote_copy(
                respond,
                respond_in.at[side],
                respond_send_sem.at[side],
                respond_recv_sem.at[side],
                device_id=(me, dest),
                device_id_type=MESH,
            )
        )
        answers[-1].start()
    lifted = lifted * factor + dot(spread[0:128, :], dense[...])
    spread[128:256, :] = lifted.astype(BF16)
    lifted = lifted * factor + dot(spread[128:256, :], dense[...])
    spread[256:384, :] = lifted.astype(BF16)
    for e in range(elems):
        for q in range(2):
            lanes = slice(128 * q, 128 * q + 128)
            even, odd = split(slope[e, 0, :, lanes].astype(F32), slope[e, 1, :, lanes].astype(F32))
            weights[e, :, 256 * q : 256 * q + 128] = even.astype(BF16)
            weights[e, :, 256 * q + 128 : 256 * q + 256] = odd.astype(BF16)

    tail = half + 16
    flux_c[tail:, :] = jnp.zeros((flux_c.shape[0] - tail, 256), BF16)

    def flight1(peer, pair):
        rows = pl.ds(pl.multiple_of(peer * mode_count, mode_count), mode_count)
        return pltpu.make_async_remote_copy(
            send1.at[peer, pair],
            recv1.at[pair, :, rows, :],
            send1_sem.at[pair, peer],
            recv1_sem.at[pair, peer],
            device_id=(peer, patch),
            device_id_type=MESH,
        )

    def flight2(peer, incoming, pair):
        rows = pl.ds(pl.multiple_of(peer * mode_count, mode_count), mode_count)
        planes = pl.ds(2 * pair, 2 - pair)
        return pltpu.make_async_remote_copy(
            send2.at[planes, rows, :],
            recv2.at[me, planes],
            send2_sem.at[pair, peer],
            recv2_sem.at[pair, incoming],
            device_id=(peer, patch),
            device_id_type=MESH,
        )

    wet = jnp.where(home < live_ref[0, 0], scale * scale, 0.0).astype(F32)
    span = ring * mode_count
    for pair in (1, 0):
        lanes = slice(128 * pair, 128 * pair + 128)
        for turn in ORDER:
            quarter = lax.rem(home + elems - turn, elems)
            for source in mates(quarter)[: ring if turn else ring - 1]:
                flight1(source, pair).wait_recv()
            if turn == 0:
                owns[pair].wait()
            depth = pl.ds(pl.multiple_of(quarter * span, span), span)
            for first, count in ((0, 512), (512, 512), (1024, 512), (1536, 16)):
                rows = slice(first, first + count)
                even = dot(out_table[0, rows, depth], recv1[pair, 0, depth, :])
                odd = dot(out_table[1, rows, depth], recv1[pair, 1, depth, :])
                if turn != ORDER[0]:
                    even = even + phys[0, rows, :]
                    odd = odd + phys[1, rows, :]
                if turn != ORDER[-1]:
                    phys[0, rows, :] = even
                    phys[1, rows, :] = odd
                    continue
                mask = lax.broadcasted_iota(jnp.int32, (count, 128), 1) < 64
                flux = []
                for mirror, field in enumerate((even + odd, even - odd)):
                    if pair:
                        turned = pltpu.roll(field, 64, 1)
                        warm[mirror, rows, :] = jnp.where(mask, turned, field) * wet
                        flux.append(field * turned * wet)
                    else:
                        flux.append(field * warm[mirror, rows, :])
                flux_c[rows, lanes] = (flux[0] + flux[1]).astype(BF16)
                if count > 16:
                    flux_s[rows, lanes] = (flux[0] - flux[1]).astype(BF16)
        mask = lax.broadcasted_iota(jnp.int32, (span, 128), 1) < 64
        for turn in BACK_ORDER:
            quarter = lax.rem(home + turn, elems)
            rows = pl.ds(pl.multiple_of(quarter * span, span), span)
            even = dot(back_table[0, rows, :], flux_c[:, lanes]) * scale
            odd = dot(back_table[1, rows, :half], flux_s[:, lanes]) * scale
            if pair:
                send2[2, rows, :] = jnp.where(mask, even, odd).astype(BF16)
            else:
                send2[0, rows, :] = even.astype(BF16)
                send2[1, rows, :] = odd.astype(BF16)
            for dest in mates(quarter)[: ring if turn else ring - 1]:
                flight2(dest, me, pair).start()
        planes = pl.ds(2 * pair, 2 - pair)
        owns[pair] = pltpu.make_async_copy(
            send2.at[planes, my_rows, :], recv2.at[me, planes], own_sem.at[2 + pair]
        )
        owns[pair].start()
    for k in range(1, parts):
        for pair in range(2):
            flight1(lax.rem(me + k, parts), pair).wait_send()

    wave = (lax.broadcasted_iota(jnp.int32, (mode_count, 1), 0) + me * mode_count).astype(F32)
    wave = wave / modes
    theta, delta = (4.0, 3.0)
    powers = jnp.zeros((2 * mode_count, STEPS * 128), F32)
    for turn in BACK_ORDER:
        quarter = lax.rem(home + elems - turn, elems)
        for source in mates(quarter)[: ring if turn else ring - 1]:
            for pair in range(2):
                flight2(source, source, pair).wait_recv()
        if turn == 0:
            for own in owns:
                own.wait()
        came = [recv2[quarter * ring + k] for k in range(ring)]
        plane = jnp.concatenate([b[0:2].reshape(2 * mode_count, 128) for b in came], axis=1)
        moved = dot_nt(plane, weights[quarter])
        around = [[], []]
        for t in range(2):
            cosine, sine = split(came[2 * t][2].astype(F32), came[2 * t + 1][2].astype(F32))
            around[0].append(-wave * sine)
            around[1].append(wave * cosine)
        around = jnp.concatenate([jnp.concatenate(a, axis=1) for a in around], axis=0)
        lanes = pl.ds(pl.multiple_of(quarter * nodes, nodes), nodes)
        part = heat[:, :, lanes].reshape(2 * mode_count, nodes) - 0.5 * (moved + around)
        forcing[:, lanes] = part
        part = part.astype(BF16)
        powers = powers + dot(part, pick[lanes, :])
        if turn != BACK_ORDER[-1]:
            told = dot(part, dense[lanes, :])
            applied[...] = told if turn == BACK_ORDER[0] else applied[...] + told

    sigma = theta / delta
    rho = 1.0 / sigma
    keep, take = [], []
    for step in range(STEPS):
        rho_new = 1.0 / (2.0 * sigma - rho)
        keep.append(rho_new * rho)
        take.append(2.0 * rho_new / delta)
        rho = rho_new
    (a0, a1, a2), (b0, b1, b2) = keep, take
    wave2 = jnp.concatenate([wave, wave], axis=0)
    wave2 = wave2 * wave2
    p0, p1, p2 = powers[:, 0:128], powers[:, 128:256], powers[:, 256:384]
    once = wave2 * p0 + p1
    twice = wave2 * once + wave2 * p1 + p2
    t0 = p0 / theta
    r1 = p0 - once / theta
    t1 = a0 * t0 + b0 * r1
    t2 = a1 * t1 + b1 * (r1 - ((a0 / theta + b0) * once - (b0 / theta) * twice))
    part_of = lax.broadcasted_iota(jnp.int32, (2 * mode_count, 128), 1) // (2 * edge)
    firsts = (t0, pltpu.roll(t1, 2 * edge, 1), pltpu.roll(t2, 4 * edge, 1))
    lasts = (pltpu.roll(t0, 128 - 2 * edge, 1), t1, pltpu.roll(t2, 2 * edge, 1))
    for side, (x, y, z) in enumerate((lasts, firsts)):
        tile = jnp.where(part_of == 0, x, jnp.where(part_of == 1, y, z))
        traces[side] = tile.astype(BF16)
    flights = []
    for side, dest in enumerate((right, left)):
        flights.append(
            pltpu.make_async_remote_copy(
                traces.at[side],
                halo.at[side],
                halo_send_sem.at[side],
                halo_recv_sem.at[side],
                device_id=(me, dest),
                device_id_type=MESH,
            )
        )
        flights[-1].start()

    rhs = forcing[...]
    every = wave2 + factor
    total = jnp.zeros_like(rhs)
    resid = rhs
    walk = resid / theta
    for step in range(STEPS):
        if step == 0:
            image = every * walk + (applied[...] + dot(part, dense[lanes, :])) / theta
        else:
            image = every * walk + dot(walk.astype(BF16), dense[...])
        total = total + walk
        resid = resid - image
        walk = keep[step] * walk + take[step] * resid
    result_ref[...] = (total + walk).reshape(2, mode_count, ndev)

    for answer in answers:
        answer.wait()
    below = lax.broadcasted_iota(jnp.int32, (128, 128), 0) < 2 * edge
    reply0 = jnp.where(below, respond_in[0, 0].astype(F32), respond_in[1, 0].astype(F32)).astype(BF16)
    reply1 = jnp.where(below, respond_in[0, 1].astype(F32), respond_in[1, 1].astype(F32)).astype(BF16)
    t0, t1 = t0.astype(BF16), t1.astype(BF16)
    back0 = dot(t0, reply0)
    back1 = dot(t1, reply0)
    back00 = dot(t0, reply1)
    around0 = dot(respond[0], reply0).astype(BF16)

    for k in range(1, parts):
        peer = lax.rem(me + k, parts)
        for pair in range(2):
            flight2(peer, peer, pair).wait_send()
    for flight in flights:
        flight.wait()
    from_left, from_right = halo[0].astype(F32), halo[1].astype(F32)
    mine = part_of == 0
    s0 = jnp.where(mine, from_right, pltpu.roll(from_left, 2 * edge, 1))
    s1 = jnp.where(mine, pltpu.roll(from_right, 128 - 2 * edge, 1), from_left)
    s2 = jnp.where(
        mine, pltpu.roll(from_right, 128 - 4 * edge, 1), pltpu.roll(from_left, 128 - 2 * edge, 1)
    )
    back1 = back1 + b0 * dot(s0.astype(BF16), around0)
    s1 = s1 + b0 * back0
    first = 1.0 - b0 * wave2
    s2 = s2 + (a1 * b0 + b1 * first) * back0 + b1 * (back1 - b0 * back00)
    grown = first * s0 + s1
    alpha = a1 * b0 * s0 + b1 * grown
    beta = -b1 * b0 * s0
    y0 = b0 * s0 + (1.0 + a2) * alpha + b2 * (grown - wave2 * alpha + s2)
    y1 = (1.0 + a2) * beta + b2 * (-b0 * s0 - wave2 * beta - alpha)
    y2 = -b2 * beta
    y = jnp.concatenate([y0.astype(BF16), y1.astype(BF16), y2.astype(BF16)], axis=1)
    outside = dot(y, spread[...])
    result_ref[...] = result_ref[...] + outside.reshape(2, mode_count, ndev)


def hand_over(solved_ref, result_ref, sem):
    copy = pltpu.make_async_copy(solved_ref, result_ref, sem)
    copy.start()
    copy.wait()


def per_device(
    flow_speed,
    heat_state,
    planar_slope_matrices,
    conduction_matrices,
    adjacent_partners,
    opposite_direction_flags,
    interpatch_sides,
    liquid_cells,
):
    parts = lax.axis_size("mode")
    patches = lax.axis_size("patch")
    _, _, mode_count, ndev = flow_speed.shape
    elems, nodes, _ = conduction_matrices.shape
    edge = math.isqrt(nodes)
    modes = mode_count * parts
    points = 3 * modes
    rows = points // 2 + 128
    out_table, back_table = tables(modes, points, rows)
    lift = lift_table(elems, edge)
    sizes = (parts, patches, mode_count, ndev, elems, edge, points)
    hbm = pl.BlockSpec(memory_space=pltpu.HBM)
    vmem = pl.BlockSpec(memory_space=pltpu.VMEM)
    small = (adjacent_partners, opposite_direction_flags, interpatch_sides)
    big = (
        flow_speed,
        heat_state,
        planar_slope_matrices,
        conduction_matrices,
        jnp.asarray(out_table),
        jnp.asarray(back_table),
        jnp.asarray(lift.astype(BF16)),
        jnp.asarray(lift.T.astype(BF16)),
    )
    solved = pl.pallas_call(
        functools.partial(kernel, sizes),
        out_shape=pltpu.VMEM(heat_state.shape, F32),
        in_specs=[pl.BlockSpec(memory_space=pltpu.SMEM)] + [hbm] * 11,
        out_specs=vmem,
        scratch_shapes=[pltpu.SMEM(a.shape, a.dtype) for a in small]
        + [pltpu.VMEM(a.shape, a.dtype) for a in big]
        + [
            pltpu.VMEM((parts, 2, 2, mode_count, 128), BF16),
            pltpu.VMEM((2, 2, modes, 128), BF16),
            pltpu.VMEM((2, points // 2 + 16, 128), F32),
            pltpu.VMEM((2, points // 2 + 16, 128), F32),
            pltpu.VMEM((rows, 256), BF16),
            pltpu.VMEM((points // 2, 256), BF16),
            pltpu.VMEM((3, modes, 128), BF16),
            pltpu.VMEM((parts, 3, mode_count, 128), BF16),
            pltpu.VMEM((elems, nodes, 2 * nodes), BF16),
            pltpu.VMEM((2 * mode_count, ndev), F32),
            pltpu.VMEM((2 * mode_count, ndev), F32),
            pltpu.VMEM((ndev, ndev), BF16),
            pltpu.VMEM((ndev, STEPS * 128), BF16),
            pltpu.VMEM((STEPS * 128, ndev), BF16),
            pltpu.VMEM((2, 128, 128), BF16),
            pltpu.VMEM((2, 2, 128, 128), BF16),
            pltpu.VMEM((2, 2 * mode_count, 128), BF16),
            pltpu.VMEM((2, 2 * mode_count, 128), BF16),
            pltpu.SemaphoreType.DMA((11,)),
            pltpu.SemaphoreType.DMA((4,)),
            pltpu.SemaphoreType.DMA((2, parts)),
            pltpu.SemaphoreType.DMA((2, parts)),
            pltpu.SemaphoreType.DMA((2, parts)),
            pltpu.SemaphoreType.DMA((2, parts)),
            pltpu.SemaphoreType.DMA((2,)),
            pltpu.SemaphoreType.DMA((2,)),
            pltpu.SemaphoreType.DMA((2,)),
            pltpu.SemaphoreType.DMA((2,)),
        ],
        compiler_params=pltpu.CompilerParams(
            collective_id=0, has_side_effects=True, vmem_limit_bytes=52 << 20
        ),
    )(
        liquid_cells.reshape(1, 1),
        *[pltpu.with_memory_space_constraint(a, pltpu.HBM) for a in small + big],
    )
    return pl.pallas_call(
        hand_over,
        out_shape=jax.ShapeDtypeStruct(heat_state.shape, F32),
        in_specs=[vmem],
        out_specs=hbm,
        scratch_shapes=[pltpu.SemaphoreType.DMA],
        compiler_params=pltpu.CompilerParams(vmem_limit_bytes=4 << 20),
    )(solved)


def solution(mesh):
    placed = (
        P(None, None, "mode", "patch"),
        P(None, "mode", "patch"),
        P("patch", None, None, None),
        P("patch", None, None),
        P("patch", None),
        P("patch", None),
        P("patch", None),
        P("patch"),
    )
    return jax.shard_map(
        per_device, mesh=mesh, in_specs=placed, out_specs=P(None, "mode", "patch"), check_vma=False
    )
```

```python
import functools
import math

import jax
import jax.numpy as jnp
import numpy as np
from jax import lax
from jax.experimental import pallas as pl
from jax.experimental.pallas import tpu as pltpu
from jax.sharding import PartitionSpec as P

STEPS = 3
ORDER = (1, 3, 2, 0)
MESH = pl.DeviceIdType.MESH
F32 = jnp.float32
BF16 = jnp.bfloat16


def tables(modes, points, rows):
    half = points // 2
    z = np.arange(half + 1)
    m = np.arange(modes)
    phase = (z[:, None] * m[None, :]) % points
    angle = phase.astype(np.float32) * np.float32(2.0 * math.pi / points)
    out = np.zeros((2, rows, modes), np.float32)
    out[0, : half + 1] = np.cos(angle)
    out[1, : half + 1] = -np.sin(angle)
    out = out.astype(BF16)
    back = np.swapaxes(out, 1, 2).astype(np.float32)
    back[:, :, 0] *= 0.5
    back[:, :, half] *= 0.5
    return out, np.ascontiguousarray(back).astype(BF16)


def lift_table(elems, edge):
    nodes = edge * edge
    out = np.zeros((elems * 4 * edge, elems * nodes), np.float32)
    for e in range(elems):
        for i in range(edge):
            for face, node in enumerate((i, (edge - 1) * edge + i, i * edge, i * edge + edge - 1)):
                out[(e * 4 + face) * edge + i, e * nodes + node] = 1.0
    return out


def dot(a, b):
    return jnp.dot(a, b, preferred_element_type=F32)


def dot_nt(a, b):
    return lax.dot_general(a, b, (((1,), (1,)), ((), ())), preferred_element_type=F32)


def kernel(
    sizes,
    live_ref,
    partners_hbm,
    flags_hbm,
    sides_hbm,
    flow_hbm,
    heat_hbm,
    slope_hbm,
    stiff_hbm,
    out_table_hbm,
    back_table_hbm,
    lift_hbm,
    lift_t_hbm,
    result_ref,
    partners_ref,
    flags_ref,
    sides_ref,
    flow,
    heat,
    slope,
    stiff,
    out_table,
    back_table,
    lift,
    lift_t,
    send1,
    recv1,
    phys,
    warm,
    flux_c,
    flux_s,
    send2,
    recv2,
    weights,
    forcing,
    applied,
    dense,
    pick,
    spread,
    respond,
    respond_in,
    traces,
    halo,
    load_sem,
    own_sem,
    send1_sem,
    recv1_sem,
    send2_sem,
    recv2_sem,
    halo_send_sem,
    halo_recv_sem,
    respond_send_sem,
    respond_recv_sem,
):
    parts, patches, mode_count, ndev, elems, edge, points = sizes
    modes = mode_count * parts
    nodes = edge * edge
    half = points // 2
    me = lax.axis_index("mode")
    patch = lax.axis_index("patch")
    left = lax.rem(patch + patches - 1, patches)
    right = lax.rem(patch + 1, patches)
    scale = math.sqrt(2.0 / points)

    loads = [
        pltpu.make_async_copy(src, dst, load_sem.at[i])
        for i, (src, dst) in enumerate(
            (
                (heat_hbm, heat),
                (flow_hbm.at[2], flow.at[2]),
                (flow_hbm.at[pl.ds(0, 2)], flow.at[pl.ds(0, 2)]),
                (out_table_hbm, out_table),
                (back_table_hbm, back_table),
                (slope_hbm, slope),
                (stiff_hbm, stiff),
                (lift_hbm, lift),
                (lift_t_hbm, lift_t),
                (partners_hbm, partners_ref),
                (flags_hbm, flags_ref),
                (sides_hbm, sides_ref),
            )
        )
    ]
    for load in loads[:3]:
        load.start()

    barrier = pltpu.get_barrier_semaphore()
    for k in range(1, parts):
        pl.semaphore_signal(
            barrier, inc=1, device_id=(lax.rem(me + k, parts), patch), device_id_type=MESH
        )
    for side in (left, right):
        pl.semaphore_signal(barrier, inc=1, device_id=(me, side), device_id_type=MESH)

    def split(a, b):
        mask = lax.broadcasted_iota(jnp.int32, a.shape, 1) < 64
        return (
            jnp.where(mask, a, pltpu.roll(b, 64, 1)),
            jnp.where(mask, pltpu.roll(a, 64, 1), b),
        )

    loads[0].wait()
    loads[1].wait()
    for load in loads[3:]:
        load.start()
    ring = parts // elems
    home, place = me // ring, lax.rem(me, ring)

    def mates(quarter):
        return [quarter * ring + lax.rem(place + k, ring) for k in range(1, ring + 1)]

    my_rows = pl.ds(pl.multiple_of(me * mode_count, mode_count), mode_count)
    owns = []
    for pair in (1, 0):
        if not pair:
            loads[2].wait()
        for turn in ORDER:
            quarter = lax.rem(home + turn, elems)
            for half_tile in range(2):
                tile = 2 * quarter + half_tile
                cols = pl.ds(pl.multiple_of(tile * 128, 128), 128)
                for c in range(2):
                    first = flow[2 * pair, c, :, cols].astype(F32)
                    if pair:
                        second = heat[c, :, cols].astype(BF16).astype(F32)
                    else:
                        second = flow[1, c, :, cols].astype(F32)
                    even, odd = split(first, second)
                    send1[2 * tile, pair, c] = even.astype(BF16)
                    send1[2 * tile + 1, pair, c] = odd.astype(BF16)
            if pair and turn == ORDER[0]:
                pl.semaphore_wait(barrier, parts + 1)
            for dest in mates(quarter)[: ring if turn else ring - 1]:
                pltpu.make_async_remote_copy(
                    send1.at[dest, pair],
                    recv1.at[pair, :, my_rows, :],
                    send1_sem.at[pair, dest],
                    recv1_sem.at[pair, me],
                    device_id=(dest, patch),
                    device_id_type=MESH,
                ).start()
        own = pltpu.make_async_copy(
            send1.at[me, pair], recv1.at[pair, :, my_rows, :], own_sem.at[pair]
        )
        own.start()
        owns.insert(0, own)

    for load in loads[3:]:
        load.wait()
    lane = lax.broadcasted_iota(jnp.int32, (1, 256), 1)
    group, offset = lane // edge, lane % edge
    source = jnp.full((1, 256), -1, jnp.int32)
    for e in range(elems):
        for face in range(4):
            there = jnp.where(flags_ref[e, face] == 1, edge - 1 - offset, offset)
            source = jnp.where(
                group == e * 4 + face, partners_ref[e, face] * edge + there, source
            )
    row = lax.broadcasted_iota(jnp.int32, (256, 256), 0)
    inner = jnp.where(row == source, 1.0, 0.0).astype(BF16)
    inner = dot(inner, lift[...]).astype(BF16)
    row = lax.broadcasted_iota(jnp.int32, (128, 256), 0)
    wanted = jnp.where(row < 2 * edge, 18 * edge + row, 16 * edge + row - 2 * edge)
    wanted = jnp.where(row < 4 * edge, wanted, -2)
    outer = jnp.where(wanted == source, 0.5, 0.0).astype(BF16)
    row = lax.broadcasted_iota(jnp.int32, (256, 128), 0)
    col = lax.broadcasted_iota(jnp.int32, (256, 128), 1)
    chosen = jnp.full((256, 128), -1, jnp.int32)
    for s in range(4):
        chosen = jnp.where(col // edge == s, sides_ref[0, s] * edge + col % edge, chosen)
    chosen = jnp.where(row == chosen, 1.0, 0.0).astype(BF16)
    same = lax.broadcasted_iota(jnp.int32, (nodes, nodes), 0) == lax.broadcasted_iota(
        jnp.int32, (nodes, nodes), 1
    )
    lane_diag, row_diag = [], []
    for e in range(elems):
        for g in range(elems):
            rows = slice(g * nodes, g * nodes + nodes)
            cols = slice(e * nodes, e * nodes + nodes)
            block = -0.5 * dot(lift_t[rows, :], inner[:, cols])
            if g == e:
                full = stiff[e].astype(F32)
                diagonal = jnp.where(same, full, 0.0)
                lane_diag.append(jnp.sum(diagonal, axis=0, keepdims=True))
                row_diag.append(jnp.sum(diagonal, axis=1, keepdims=True))
                block = block + (full - diagonal)
            dense[rows, cols] = block.astype(BF16)

    def own_factor(axis):
        shape = (1, ndev) if axis else (ndev, 1)
        node = lax.broadcasted_iota(jnp.int32, shape, axis)
        a, b = node // edge % edge, node % edge
        hits = (a == 0, a == edge - 1, b == 0, b == edge - 1)
        return 1.0 + sum(jnp.where(hit, 0.5, 0.0) for hit in hits)

    factor = own_factor(1) + jnp.concatenate(lane_diag, axis=1)
    row_factor = own_factor(0) + jnp.concatenate(row_diag, axis=0)
    trace = dot(lift_t[...], chosen)
    pick[:, 0:128] = trace.astype(BF16)
    trace = trace * row_factor + dot(dense[...], pick[:, 0:128])
    pick[:, 128:256] = trace.astype(BF16)
    trace = trace * row_factor + dot(dense[...], pick[:, 128:256])
    pick[:, 256:384] = trace.astype(BF16)
    lifted = dot(outer, lift[...])
    spread[0:128, :] = lifted.astype(BF16)
    respond[0] = dot(spread[0:128, :], pick[:, 0:128]).astype(BF16)
    respond[1] = dot(spread[0:128, :], pick[:, 128:256]).astype(BF16)
    answers = []
    for side, dest in enumerate((right, left)):
        answers.append(
            pltpu.make_async_remote_copy(
                respond,
                respond_in.at[side],
                respond_send_sem.at[side],
                respond_recv_sem.at[side],
                device_id=(me, dest),
                device_id_type=MESH,
            )
        )
        answers[-1].start()
    lifted = lifted * factor + dot(spread[0:128, :], dense[...])
    spread[128:256, :] = lifted.astype(BF16)
    lifted = lifted * factor + dot(spread[128:256, :], dense[...])
    spread[256:384, :] = lifted.astype(BF16)
    for e in range(elems):
        for q in range(2):
            lanes = slice(128 * q, 128 * q + 128)
            even, odd = split(slope[e, 0, :, lanes].astype(F32), slope[e, 1, :, lanes].astype(F32))
            weights[e, :, 256 * q : 256 * q + 128] = even.astype(BF16)
            weights[e, :, 256 * q + 128 : 256 * q + 256] = odd.astype(BF16)

    tail = half + 16
    flux_c[tail:, :] = jnp.zeros((flux_c.shape[0] - tail, 256), BF16)

    def flight1(peer, pair):
        rows = pl.ds(pl.multiple_of(peer * mode_count, mode_count), mode_count)
        return pltpu.make_async_remote_copy(
            send1.at[peer, pair],
            recv1.at[pair, :, rows, :],
            send1_sem.at[pair, peer],
            recv1_sem.at[pair, peer],
            device_id=(peer, patch),
            device_id_type=MESH,
        )

    def flight2(peer, incoming, pair):
        rows = pl.ds(pl.multiple_of(peer * mode_count, mode_count), mode_count)
        planes = pl.ds(2 * pair, 2 - pair)
        return pltpu.make_async_remote_copy(
            send2.at[planes, rows, :],
            recv2.at[me, planes],
            send2_sem.at[pair, peer],
            recv2_sem.at[pair, incoming],
            device_id=(peer, patch),
            device_id_type=MESH,
        )

    wet = jnp.where(home < live_ref[0, 0], scale * scale, 0.0).astype(F32)
    span = ring * mode_count
    for pair in (1, 0):
        lanes = slice(128 * pair, 128 * pair + 128)
        for turn in ORDER:
            quarter = lax.rem(home + elems - turn, elems)
            for source in mates(quarter)[: ring if turn else ring - 1]:
                flight1(source, pair).wait_recv()
            if turn == 0:
                owns[pair].wait()
            depth = pl.ds(pl.multiple_of(quarter * span, span), span)
            for first, count in ((0, 512), (512, 512), (1024, 512), (1536, 16)):
                rows = slice(first, first + count)
                even = dot(out_table[0, rows, depth], recv1[pair, 0, depth, :])
                odd = dot(out_table[1, rows, depth], recv1[pair, 1, depth, :])
                if turn != ORDER[0]:
                    even = even + phys[0, rows, :]
                    odd = odd + phys[1, rows, :]
                if turn != ORDER[-1]:
                    phys[0, rows, :] = even
                    phys[1, rows, :] = odd
                    continue
                mask = lax.broadcasted_iota(jnp.int32, (count, 128), 1) < 64
                flux = []
                for mirror, field in enumerate((even + odd, even - odd)):
                    if pair:
                        turned = pltpu.roll(field, 64, 1)
                        warm[mirror, rows, :] = jnp.where(mask, turned, field) * wet
                        flux.append(field * turned * wet)
                    else:
                        flux.append(field * warm[mirror, rows, :])
                flux_c[rows, lanes] = (flux[0] + flux[1]).astype(BF16)
                if count > 16:
                    flux_s[rows, lanes] = (flux[0] - flux[1]).astype(BF16)
        mask = lax.broadcasted_iota(jnp.int32, (span, 128), 1) < 64
        for turn in ORDER:
            quarter = lax.rem(home + turn, elems)
            rows = pl.ds(pl.multiple_of(quarter * span, span), span)
            even = dot(back_table[0, rows, :], flux_c[:, lanes]) * scale
            odd = dot(back_table[1, rows, :half], flux_s[:, lanes]) * scale
            if pair:
                send2[2, rows, :] = jnp.where(mask, even, odd).astype(BF16)
            else:
                send2[0, rows, :] = even.astype(BF16)
                send2[1, rows, :] = odd.astype(BF16)
            for dest in mates(quarter)[: ring if turn else ring - 1]:
                flight2(dest, me, pair).start()
        planes = pl.ds(2 * pair, 2 - pair)
        owns[pair] = pltpu.make_async_copy(
            send2.at[planes, my_rows, :], recv2.at[me, planes], own_sem.at[2 + pair]
        )
        owns[pair].start()
    for k in range(1, parts):
        for pair in range(2):
            flight1(lax.rem(me + k, parts), pair).wait_send()

    wave = (lax.broadcasted_iota(jnp.int32, (mode_count, 1), 0) + me * mode_count).astype(F32)
    wave = wave / modes
    theta, delta = (4.0, 3.0)
    for turn in ORDER:
        quarter = lax.rem(home + elems - turn, elems)
        for source in mates(quarter)[: ring if turn else ring - 1]:
            flight2(source, source, 1).wait_recv()
        if turn == 0:
            owns[1].wait()
        around = [[], []]
        for t in range(2):
            came = [recv2[quarter * ring + 2 * t + k, 2].astype(F32) for k in range(2)]
            cosine, sine = split(*came)
            around[0].append(-wave * sine)
            around[1].append(wave * cosine)
        around = jnp.concatenate([jnp.concatenate(a, axis=1) for a in around], axis=0)
        lanes = pl.ds(pl.multiple_of(quarter * nodes, nodes), nodes)
        forcing[:, lanes] = heat[:, :, lanes].reshape(2 * mode_count, nodes) - 0.5 * around
    powers = jnp.zeros((2 * mode_count, STEPS * 128), F32)
    for turn in ORDER:
        quarter = lax.rem(home + elems - turn, elems)
        for source in mates(quarter)[: ring if turn else ring - 1]:
            flight2(source, source, 0).wait_recv()
        if turn == 0:
            owns[0].wait()
        came = [
            recv2[quarter * ring + k, 0:2].reshape(2 * mode_count, 128) for k in range(ring)
        ]
        moved = dot_nt(jnp.concatenate(came, axis=1), weights[quarter])
        lanes = pl.ds(pl.multiple_of(quarter * nodes, nodes), nodes)
        part = forcing[:, lanes] - 0.5 * moved
        forcing[:, lanes] = part
        part = part.astype(BF16)
        powers = powers + dot(part, pick[lanes, :])
        if turn != ORDER[-1]:
            told = dot(part, dense[lanes, :])
            applied[...] = told if turn == ORDER[0] else applied[...] + told

    sigma = theta / delta
    rho = 1.0 / sigma
    keep, take = [], []
    for step in range(STEPS):
        rho_new = 1.0 / (2.0 * sigma - rho)
        keep.append(rho_new * rho)
        take.append(2.0 * rho_new / delta)
        rho = rho_new
    (a0, a1, a2), (b0, b1, b2) = keep, take
    wave2 = jnp.concatenate([wave, wave], axis=0)
    wave2 = wave2 * wave2
    p0, p1, p2 = powers[:, 0:128], powers[:, 128:256], powers[:, 256:384]
    once = wave2 * p0 + p1
    twice = wave2 * once + wave2 * p1 + p2
    t0 = p0 / theta
    r1 = p0 - once / theta
    t1 = a0 * t0 + b0 * r1
    t2 = a1 * t1 + b1 * (r1 - ((a0 / theta + b0) * once - (b0 / theta) * twice))
    part_of = lax.broadcasted_iota(jnp.int32, (2 * mode_count, 128), 1) // (2 * edge)
    firsts = (t0, pltpu.roll(t1, 2 * edge, 1), pltpu.roll(t2, 4 * edge, 1))
    lasts = (pltpu.roll(t0, 128 - 2 * edge, 1), t1, pltpu.roll(t2, 2 * edge, 1))
    for side, (x, y, z) in enumerate((lasts, firsts)):
        tile = jnp.where(part_of == 0, x, jnp.where(part_of == 1, y, z))
        traces[side] = tile.astype(BF16)
    flights = []
    for side, dest in enumerate((right, left)):
        flights.append(
            pltpu.make_async_remote_copy(
                traces.at[side],
                halo.at[side],
                halo_send_sem.at[side],
                halo_recv_sem.at[side],
                device_id=(me, dest),
                device_id_type=MESH,
            )
        )
        flights[-1].start()

    rhs = forcing[...]
    every = wave2 + factor
    total = jnp.zeros_like(rhs)
    resid = rhs
    walk = resid / theta
    for step in range(STEPS):
        if step == 0:
            image = every * walk + (applied[...] + dot(part, dense[lanes, :])) / theta
        else:
            image = every * walk + dot(walk.astype(BF16), dense[...])
        total = total + walk
        resid = resid - image
        walk = keep[step] * walk + take[step] * resid
    result_ref[...] = (total + walk).reshape(2, mode_count, ndev)

    for answer in answers:
        answer.wait()
    below = lax.broadcasted_iota(jnp.int32, (128, 128), 0) < 2 * edge
    reply0 = jnp.where(below, respond_in[0, 0].astype(F32), respond_in[1, 0].astype(F32)).astype(BF16)
    reply1 = jnp.where(below, respond_in[0, 1].astype(F32), respond_in[1, 1].astype(F32)).astype(BF16)
    t0, t1 = t0.astype(BF16), t1.astype(BF16)
    back0 = dot(t0, reply0)
    back1 = dot(t1, reply0)
    back00 = dot(t0, reply1)
    around0 = dot(respond[0], reply0).astype(BF16)

    for k in range(1, parts):
        peer = lax.rem(me + k, parts)
        for pair in range(2):
            flight2(peer, peer, pair).wait_send()
    for flight in flights:
        flight.wait()
    from_left, from_right = halo[0].astype(F32), halo[1].astype(F32)
    mine = part_of == 0
    s0 = jnp.where(mine, from_right, pltpu.roll(from_left, 2 * edge, 1))
    s1 = jnp.where(mine, pltpu.roll(from_right, 128 - 2 * edge, 1), from_left)
    s2 = jnp.where(
        mine, pltpu.roll(from_right, 128 - 4 * edge, 1), pltpu.roll(from_left, 128 - 2 * edge, 1)
    )
    back1 = back1 + b0 * dot(s0.astype(BF16), around0)
    s1 = s1 + b0 * back0
    first = 1.0 - b0 * wave2
    s2 = s2 + (a1 * b0 + b1 * first) * back0 + b1 * (back1 - b0 * back00)
    grown = first * s0 + s1
    alpha = a1 * b0 * s0 + b1 * grown
    beta = -b1 * b0 * s0
    y0 = b0 * s0 + (1.0 + a2) * alpha + b2 * (grown - wave2 * alpha + s2)
    y1 = (1.0 + a2) * beta + b2 * (-b0 * s0 - wave2 * beta - alpha)
    y2 = -b2 * beta
    y = jnp.concatenate([y0.astype(BF16), y1.astype(BF16), y2.astype(BF16)], axis=1)
    outside = dot(y, spread[...])
    result_ref[...] = result_ref[...] + outside.reshape(2, mode_count, ndev)


def hand_over(solved_ref, result_ref, sem):
    copy = pltpu.make_async_copy(solved_ref, result_ref, sem)
    copy.start()
    copy.wait()


def per_device(
    flow_speed,
    heat_state,
    planar_slope_matrices,
    conduction_matrices,
    adjacent_partners,
    opposite_direction_flags,
    interpatch_sides,
    liquid_cells,
):
    parts = lax.axis_size("mode")
    patches = lax.axis_size("patch")
    _, _, mode_count, ndev = flow_speed.shape
    elems, nodes, _ = conduction_matrices.shape
    edge = math.isqrt(nodes)
    modes = mode_count * parts
    points = 3 * modes
    rows = points // 2 + 128
    out_table, back_table = tables(modes, points, rows)
    lift = lift_table(elems, edge)
    sizes = (parts, patches, mode_count, ndev, elems, edge, points)
    hbm = pl.BlockSpec(memory_space=pltpu.HBM)
    vmem = pl.BlockSpec(memory_space=pltpu.VMEM)
    small = (adjacent_partners, opposite_direction_flags, interpatch_sides)
    big = (
        flow_speed,
        heat_state,
        planar_slope_matrices,
        conduction_matrices,
        jnp.asarray(out_table),
        jnp.asarray(back_table),
        jnp.asarray(lift.astype(BF16)),
        jnp.asarray(lift.T.astype(BF16)),
    )
    solved = pl.pallas_call(
        functools.partial(kernel, sizes),
        out_shape=pltpu.VMEM(heat_state.shape, F32),
        in_specs=[pl.BlockSpec(memory_space=pltpu.SMEM)] + [hbm] * 11,
        out_specs=vmem,
        scratch_shapes=[pltpu.SMEM(a.shape, a.dtype) for a in small]
        + [pltpu.VMEM(a.shape, a.dtype) for a in big]
        + [
            pltpu.VMEM((parts, 2, 2, mode_count, 128), BF16),
            pltpu.VMEM((2, 2, modes, 128), BF16),
            pltpu.VMEM((2, points // 2 + 16, 128), F32),
            pltpu.VMEM((2, points // 2 + 16, 128), F32),
            pltpu.VMEM((rows, 256), BF16),
            pltpu.VMEM((points // 2, 256), BF16),
            pltpu.VMEM((3, modes, 128), BF16),
            pltpu.VMEM((parts, 3, mode_count, 128), BF16),
            pltpu.VMEM((elems, nodes, 2 * nodes), BF16),
            pltpu.VMEM((2 * mode_count, ndev), F32),
            pltpu.VMEM((2 * mode_count, ndev), F32),
            pltpu.VMEM((ndev, ndev), BF16),
            pltpu.VMEM((ndev, STEPS * 128), BF16),
            pltpu.VMEM((STEPS * 128, ndev), BF16),
            pltpu.VMEM((2, 128, 128), BF16),
            pltpu.VMEM((2, 2, 128, 128), BF16),
            pltpu.VMEM((2, 2 * mode_count, 128), BF16),
            pltpu.VMEM((2, 2 * mode_count, 128), BF16),
            pltpu.SemaphoreType.DMA((12,)),
            pltpu.SemaphoreType.DMA((4,)),
            pltpu.SemaphoreType.DMA((2, parts)),
            pltpu.SemaphoreType.DMA((2, parts)),
            pltpu.SemaphoreType.DMA((2, parts)),
            pltpu.SemaphoreType.DMA((2, parts)),
            pltpu.SemaphoreType.DMA((2,)),
            pltpu.SemaphoreType.DMA((2,)),
            pltpu.SemaphoreType.DMA((2,)),
            pltpu.SemaphoreType.DMA((2,)),
        ],
        compiler_params=pltpu.CompilerParams(
            collective_id=0, has_side_effects=True, vmem_limit_bytes=52 << 20
        ),
    )(
        liquid_cells.reshape(1, 1),
        *[pltpu.with_memory_space_constraint(a, pltpu.HBM) for a in small + big],
    )
    return pl.pallas_call(
        hand_over,
        out_shape=jax.ShapeDtypeStruct(heat_state.shape, F32),
        in_specs=[vmem],
        out_specs=hbm,
        scratch_shapes=[pltpu.SemaphoreType.DMA],
        compiler_params=pltpu.CompilerParams(vmem_limit_bytes=4 << 20),
    )(solved)


def solution(mesh):
    placed = (
        P(None, None, "mode", "patch"),
        P(None, "mode", "patch"),
        P("patch", None, None, None),
        P("patch", None, None),
        P("patch", None),
        P("patch", None),
        P("patch", None),
        P("patch"),
    )
    return jax.shard_map(
        per_device, mesh=mesh, in_specs=placed, out_specs=P(None, "mode", "patch"), check_vma=False
    )
```
